32 devices in a mesh: dp: 8 (over y, x, core), tensor: 4 (over z).
Axes of the slice: x: 2, y: 2, z: 4, core: 2. Of those that a mesh axis runs over, the one named last changes fastest.
Arguments:
- tokens: bfloat16 [8192, 2048], P(('dp', 'tensor')), may hold values from -6 to 6
- norm_attn: bfloat16 [2048], P('dp'), may hold values from 0.5 to 1.5
- w_query: bfloat16 [2048, 2048], P('dp', 'tensor'), may hold values from -0.125 to 0.125
- key_matrix: bfloat16 [2048, 1024], P('dp', 'tensor'), may hold values from -0.125 to 0.125
- value_matrix: bfloat16 [2048, 1024], P('dp', 'tensor'), may hold values from -0.125 to 0.125
- gain_query: bfloat16 [128], P('dp'), may hold values from 0.25 to 1.75
- gain_key: bfloat16 [128], P('dp'), may hold values from 0.25 to 1.75
- w_output: bfloat16 [2048, 2048], P('tensor', 'dp'), may hold values from -0.5 to 0.5
- norm_ffn: bfloat16 [2048], P('dp'), may hold values from 0.5 to 1.5
- w_gate: bfloat16 [2048, 6144], P('dp', 'tensor'), may hold values from -0.125 to 0.125
- w_up: bfloat16 [2048, 6144], P('dp', 'tensor'), may hold values from -0.125 to 0.125
- w_down: bfloat16 [6144, 2048], P('tensor', 'dp'), may hold values from -0.078125 to 0.078125
- cotangent: bfloat16 [8192, 2048], P(('dp', 'tensor')), may hold values from -6 to 6
- lengths: int32 [8], replicated, may hold values from 769 to 1024, as said below
- deal_order: int32 [8], replicated, may hold values from 0 to 7, as said below
Outputs:
- block_out: bfloat16 [8192, 2048], P(('dp', 'tensor'))
- grad_tokens: bfloat16 [8192, 2048], P(('dp', 'tensor'))
- grad_norm_attn: float32 [2048], P('dp')
- grad_query: float32 [2048, 2048], P('dp', 'tensor')
- grad_key: float32 [2048, 1024], P('dp', 'tensor')
- grad_value: float32 [2048, 1024], P('dp', 'tensor')
- grad_gain_query: float32 [128], P('dp')
- grad_gain_key: float32 [128], P('dp')
- grad_output: float32 [2048, 2048], P('tensor', 'dp')
- grad_norm_ffn: float32 [2048], P('dp')
- grad_gate: float32 [2048, 6144], P('dp', 'tensor')
- grad_up: float32 [2048, 6144], P('dp', 'tensor')
- grad_down: float32 [6144, 2048], P('tensor', 'dp')
The draws below stay inside these ranges and needn't reach their ends.
Inputs may be any that keep to these rules, and one draw needn't show every extreme that they name: Data group g takes sequence deal_order[g]; deal_order is a permutation. `lengths`: one group's sequence fills all 1024 of its rows and another's leaves 256 - 1 rows of padding.
All inputs are finite; a program needn't handle non-finite values.
Results may differ from the reference program's by a relative error of at most 0.023.
Values may be sent and summed in bfloat16 or wider, within the bound.
No kernel may reach another device: no remote copies, remote signals or barrier semaphores. Data moves between devices by JAX's collectives and lax.ppermute only.
A program may use at most 192 MiB of HBM per device.

```python
import jax
import jax.numpy as jnp
from jax import lax

MODEL_WIDTH = 2048
QUERY_HEADS = 16
KEY_VALUE_HEADS = 8
HEAD_SIZE = 128
FF = 6144
TOK_DEV = 256
GROUP_TOK = 1024
TOKENS = 8192
NSEQ = 8
N_DP = 8


def dealt(key):
    base_key = jax.random.fold_in(key, 4242)
    splits = jax.random.split(base_key, 4)
    leftover = jax.random.randint(splits[0], (NSEQ,), 0, TOK_DEV)
    chosen = jax.random.randint(splits[1], (), 0, NSEQ)
    other = (chosen + 1 + jax.random.randint(splits[2], (), 0, NSEQ - 1)) % NSEQ
    slots = jnp.arange(NSEQ)
    leftover = jnp.where(slots == chosen, 0, jnp.where(slots == other, TOK_DEV - 1, leftover))
    placed = (GROUP_TOK - leftover).astype(jnp.int32)
    dealing = jax.random.permutation(splits[3], NSEQ).astype(jnp.int32)
    length_table = jnp.zeros((NSEQ,), jnp.int32).at[dealing].set(placed)
    return (dealing, length_table)


def draw_lengths(key, part):
    return dealt(key)[1]


def draw_deal_order(key, part):
    return dealt(key)[0]


def spiked(result, stream_key, source, target, parts, factor):
    def block_of(dim):
        return (jnp.arange(result.shape[dim]) // (result.shape[dim] // parts)).reshape((-1,) + (1,) * (result.ndim - 1 - dim))

    near = jax.random.permutation(stream_key, parts)[block_of(target)]
    second = (block_of(target) + parts // 2) % parts
    return jnp.where((block_of(source) == near) | (block_of(source) == second), factor * result, result)


def levels(stream_key, extent, shards, least, top_value):
    loudness = 1.0
    for axis_at, shards_of in shards:
        heights = jax.random.uniform(jax.random.fold_in(jax.random.fold_in(stream_key, 6), axis_at), (shards_of,), jnp.float32, least / len(shards), top_value / len(shards))
        loudness = loudness * jnp.repeat(jnp.exp(heights), extent[axis_at] // shards_of).reshape((-1,) + (1,) * (len(extent) - 1 - axis_at))
    return loudness


def bell_draw(rng, dims, deviation, bound, cuts=(), held_as=jnp.bfloat16):
    factor_of = levels(rng, dims, cuts, -0.22, 0.18) if cuts else 1.0
    array = jax.random.normal(rng, dims, jnp.float32) * deviation * factor_of
    return jnp.minimum(jnp.maximum(array, -bound), bound).astype(held_as)


def noise_with(key, shape, width, reach, shards, heavy, held_as=jnp.bfloat16):
    drawn = width * jax.random.normal(key, shape, jnp.float32)
    if shards:
        drawn = drawn * levels(key, shape, shards, -0.22, 0.18)
    return jnp.clip(spiked(drawn, jax.random.fold_in(key, 3), *heavy), -reach, reach).astype(held_as)


def setup_inputs(seed: int = 0) -> dict:
    streams_of = jax.random.split(jax.random.key(seed), 16)
    return {
        "tokens": noise_with(streams_of[0], (TOKENS, MODEL_WIDTH), 1.0, 6.0, ((0, 32),), (0, 1, 32, 2.75)),
        "norm_attn": jnp.clip(1.0 + 0.1 * jax.random.normal(streams_of[1], (MODEL_WIDTH,), jnp.float32), 0.5, 1.5).astype(jnp.bfloat16),
        "w_query": bell_draw(streams_of[2], (MODEL_WIDTH, QUERY_HEADS * HEAD_SIZE), MODEL_WIDTH ** -0.5, 0.125, ((0, 8), (1, 4))),
        "key_matrix": bell_draw(streams_of[3], (MODEL_WIDTH, KEY_VALUE_HEADS * HEAD_SIZE), MODEL_WIDTH ** -0.5, 0.125, ((0, 8), (1, 4))),
        "value_matrix": bell_draw(streams_of[4], (MODEL_WIDTH, KEY_VALUE_HEADS * HEAD_SIZE), MODEL_WIDTH ** -0.5, 0.125, ((0, 8), (1, 4))),
        "gain_query": jnp.clip(1.0 + 0.15 * jax.random.normal(streams_of[5], (HEAD_SIZE,), jnp.float32), 0.25, 1.75).astype(jnp.bfloat16),
        "gain_key": jnp.clip(1.0 + 0.15 * jax.random.normal(streams_of[6], (HEAD_SIZE,), jnp.float32), 0.25, 1.75).astype(jnp.bfloat16),
        "w_output": bell_draw(streams_of[7], (QUERY_HEADS * HEAD_SIZE, MODEL_WIDTH), (QUERY_HEADS * HEAD_SIZE // 16) ** -0.5, 0.5, ((0, 4), (1, 8))),
        "norm_ffn": jnp.clip(1.0 + 0.1 * jax.random.normal(streams_of[8], (MODEL_WIDTH,), jnp.float32), 0.5, 1.5).astype(jnp.bfloat16),
        "w_gate": bell_draw(streams_of[9], (MODEL_WIDTH, FF), MODEL_WIDTH ** -0.5, 0.125, ((0, 8), (1, 4))),
        "w_up": bell_draw(streams_of[10], (MODEL_WIDTH, FF), MODEL_WIDTH ** -0.5, 0.125, ((0, 8), (1, 4))),
        "w_down": bell_draw(streams_of[11], (FF, MODEL_WIDTH), FF ** -0.5, 0.078125, ((0, 4), (1, 8))),
        "cotangent": bell_draw(streams_of[12], (TOKENS, MODEL_WIDTH), 1.0, 6.0, ((0, 32),)),
        "lengths": draw_lengths(jax.random.fold_in(streams_of[15], 71), 0),
        "deal_order": draw_deal_order(jax.random.fold_in(streams_of[15], 71), 0),
    }


norm_eps = 1e-06
rope_base = 1000000.0

@jax.custom_vjp
def lower_precision(v):
    return lax.optimization_barrier(v.astype(jnp.bfloat16)).astype(jnp.float32)

@jax.custom_vjp
def lower_precision_back(v):
    return v

def low_keep(v):
    return (lower_precision(v), None)

def low_pass(kept, grad):
    return (grad,)

def back_keep(v):
    return (v, None)

def back_low(kept, grad):
    return (lower_precision(grad),)
lower_precision.defvjp(low_keep, low_pass)
lower_precision_back.defvjp(back_keep, back_low)

def rms_scale(value_vectors):
    return lax.rsqrt(lax.optimization_barrier(jnp.mean(value_vectors * value_vectors, axis=-1, keepdims=True)) + norm_eps)

def rope_tables(position):
    half_dim = HEAD_SIZE // 2
    inverse_freq = rope_base ** (-2.0 * jnp.arange(half_dim, dtype=jnp.float32) / HEAD_SIZE)
    angles = position.astype(jnp.float32)[:, None] * inverse_freq[None, :]
    angles = jnp.concatenate([angles, angles], axis=1)
    return (jnp.cos(angles), jnp.sin(angles))

def rotate_half(value_vectors):
    half_dim = value_vectors.shape[-1] // 2
    return jnp.concatenate([-value_vectors[..., half_dim:], value_vectors[..., :half_dim]], axis=-1)

def group_layout(lengths, deal_order, group_id, count_of_rows):
    slots = jnp.arange(deal_order.shape[0], dtype=jnp.int32)
    seq_taken = jnp.sum(jnp.where(slots == group_id, deal_order, 0)).astype(jnp.int32)
    seq_len = jnp.sum(jnp.where(slots == seq_taken, lengths, 0)).astype(jnp.int32)
    row_index = jnp.arange(count_of_rows, dtype=jnp.int32)
    segment = (row_index >= seq_len).astype(jnp.int32)
    seg_start = jnp.where(segment == 0, 0, seq_len).astype(jnp.int32)
    return (segment, row_index - seg_start, row_index < seq_len)

def matrix_multiply(left, right):
    return jnp.dot(left, right, precision=lax.Precision.HIGHEST)

def forward_layer(token_rows, weights, segment, position, live_rows):
    norm_attn, w_query, key_matrix, value_matrix, gain_query, gain_key, w_output, norm_ffn, w_gate, w_up, w_down = weights
    count_of_rows = token_rows.shape[0]
    attention_normed_input = lower_precision(token_rows * rms_scale(token_rows) * norm_attn)
    q_pre = lower_precision_back(matrix_multiply(attention_normed_input, w_query)).reshape(count_of_rows, QUERY_HEADS, HEAD_SIZE)
    key_before_norm = lower_precision_back(matrix_multiply(attention_normed_input, key_matrix)).reshape(count_of_rows, KEY_VALUE_HEADS, HEAD_SIZE)
    value_vectors = lower_precision_back(lower_precision(matrix_multiply(attention_normed_input, value_matrix))).reshape(count_of_rows, KEY_VALUE_HEADS, HEAD_SIZE)
    cosine_table, sine_table = rope_tables(position)
    cosine_table = cosine_table[:, None, :]
    sine_table = sine_table[:, None, :]
    q_unit = q_pre * rms_scale(q_pre) * gain_query
    queries = lower_precision(q_unit * cosine_table + rotate_half(q_unit) * sine_table)
    k_unit = key_before_norm * rms_scale(key_before_norm) * gain_key
    key_rot = lower_precision(k_unit * cosine_table + rotate_half(k_unit) * sine_table)
    rows_per_group = QUERY_HEADS // KEY_VALUE_HEADS
    keys_all = jnp.repeat(key_rot, rows_per_group, axis=1)
    values_all = jnp.repeat(value_vectors, rows_per_group, axis=1)
    scores = jnp.einsum('qhd,khd->hqk', queries, keys_all, precision=lax.Precision.HIGHEST) * HEAD_SIZE ** (-0.5)
    scores = lower_precision_back(scores)
    row_index = jnp.arange(count_of_rows, dtype=jnp.int32)
    allowed = (segment[:, None] == segment[None, :]) & (row_index[None, :] <= row_index[:, None])
    scores = jnp.where(allowed[None], scores, -1e+30)
    attn_probs = lower_precision(jax.nn.softmax(scores, axis=-1))
    context = jnp.einsum('hqk,khd->qhd', attn_probs, values_all, precision=lax.Precision.HIGHEST)
    context = lower_precision_back(lower_precision(context.reshape(count_of_rows, QUERY_HEADS * HEAD_SIZE)))
    hidden = token_rows + lower_precision_back(matrix_multiply(context, w_output))
    normed_ffn = lower_precision(hidden * rms_scale(hidden) * norm_ffn)
    gate_proj = lower_precision_back(matrix_multiply(normed_ffn, w_gate))
    up_proj = lower_precision_back(matrix_multiply(normed_ffn, w_up))
    activation = lower_precision(jax.nn.silu(gate_proj) * up_proj)
    block_rows = hidden + lower_precision_back(matrix_multiply(activation, w_down))
    return block_rows * live_rows[:, None].astype(jnp.float32)

def reference(tokens, norm_attn, w_query, key_matrix, value_matrix, gain_query, gain_key, w_output, norm_ffn, w_gate, w_up, w_down, cotangent, lengths, deal_order):
    weights = tuple((weight_item.astype(jnp.float32) for weight_item in (norm_attn, w_query, key_matrix, value_matrix, gain_query, gain_key, w_output, norm_ffn, w_gate, w_up, w_down)))
    token_groups = tokens.astype(jnp.float32).reshape(N_DP, GROUP_TOK, MODEL_WIDTH)
    grad_groups = cotangent.astype(jnp.float32).reshape(N_DP, GROUP_TOK, MODEL_WIDTH)

    def one_group(totals, inputs):
        group_id, token_rows, grad_rows = inputs
        segment, position, live_rows = group_layout(lengths, deal_order, group_id, GROUP_TOK)

        def layer_of(token_arg, *weight_args):
            return forward_layer(token_arg, weight_args, segment, position, live_rows)
        block_rows, pullback = jax.vjp(layer_of, token_rows, *weights)
        gradients = pullback(grad_rows)
        totals = tuple((running + gradient for running, gradient in zip(totals, gradients[1:])))
        return (totals, (block_rows, gradients[0]))
    zeros_init = tuple((jnp.zeros_like(weight_item) for weight_item in weights))
    totals, (block_rows, grad_rows) = lax.scan(one_group, zeros_init, (jnp.arange(N_DP, dtype=jnp.int32), token_groups, grad_groups))
    return (block_rows.reshape(TOKENS, MODEL_WIDTH).astype(jnp.bfloat16), grad_rows.reshape(TOKENS, MODEL_WIDTH).astype(jnp.bfloat16), totals[0], totals[1], totals[2], totals[3], totals[4], totals[5], totals[6], totals[7], totals[8], totals[9], totals[10])
```

```python
import functools

import jax
import jax.numpy as jnp
from jax import lax
from jax.experimental import pallas as pl
from jax.experimental.pallas import tpu as pltpu
from jax.sharding import PartitionSpec as P

QUERY_HEADS = 16
KEY_VALUE_HEADS = 8
HEAD_SIZE = 128

norm_eps = 1e-06
rope_base = 1000000.0
score_scale = HEAD_SIZE ** (-0.5)
f32 = jnp.float32
bf16 = jnp.bfloat16
WAYS = 4
ROOM = 58 << 20


def nn(left, right):
    return lax.dot_general(left, right, (((1,), (0,)), ((), ())), preferred_element_type=f32)


def nt(left, right):
    return lax.dot_general(left, right, (((1,), (1,)), ((), ())), preferred_element_type=f32)


def tn(left, right):
    return lax.dot_general(left, right, (((0,), (0,)), ((), ())), preferred_element_type=f32)


def rms_scale(value_vectors):
    return lax.rsqrt(jnp.mean(value_vectors * value_vectors, axis=-1, keepdims=True) + norm_eps)


def norm_back(d_unit, pre_values, pre_scale, gain_values):
    mixed_terms = gain_values * d_unit
    return pre_scale * mixed_terms - pre_values * pre_scale**3 * jnp.mean(
        mixed_terms * pre_values, axis=-1, keepdims=True
    )


def rope_tables(position):
    half_dim = HEAD_SIZE // 2
    inverse_freq = rope_base ** (-2.0 * jnp.arange(half_dim, dtype=f32) / HEAD_SIZE)
    angles = position.astype(f32)[:, None] * inverse_freq[None, :]
    cosine, sine = jnp.cos(angles), jnp.sin(angles)
    return jnp.concatenate([cosine, cosine], axis=1), jnp.concatenate([-sine, sine], axis=1)


def sequence_length(lengths, deal_order, group_id):
    slots = jnp.arange(deal_order.shape[0], dtype=jnp.int32)
    seq_taken = jnp.sum(jnp.where(slots == group_id, deal_order, 0))
    return jnp.sum(jnp.where(slots == seq_taken, lengths, 0))


def shift_by(value, step):
    return lax.ppermute(value, "tensor", [(i, (i + step) % WAYS) for i in range(WAYS)])


def hop(value):
    return shift_by(value, 1)


def together(*values):
    return lax.optimization_barrier(values)


def add(block, arrived):
    return (block.astype(f32) + arrived.astype(f32)).astype(bf16)


def whole(shape, index=None):
    rank = len(shape)
    place = index if index is not None else (0,) * rank
    return pl.BlockSpec(shape, lambda *_: place, pipeline_mode=pl.Buffered(1))


def call(kernel, grid, in_specs, outs, out_specs, scratch=(), flops=0, size=0, exps=0):
    return pl.pallas_call(
        kernel,
        grid=grid,
        in_specs=in_specs,
        out_shape=[jax.ShapeDtypeStruct(s, d) for s, d in outs],
        out_specs=out_specs,
        scratch_shapes=list(scratch),
        compiler_params=pltpu.CompilerParams(vmem_limit_bytes=ROOM),
        cost_estimate=pl.CostEstimate(flops=flops, bytes_accessed=size, transcendentals=exps),
    )


def pick_slot(step, slots, x_s):
    for j, ref in enumerate(slots):

        @pl.when(step == j)
        def _():
            x_s[...] = ref[...]


def project_kernel(own, below, far, above, w, gain, gain_q, gain_k, cos, sin, normed, qkv, pre, x_s):
    pick_slot(pl.program_id(0), (own, below, far, above), x_s)
    x = x_s[...].astype(f32)
    n = (x * rms_scale(x) * gain[...]).astype(bf16)
    normed[...] = n
    projected = nn(n, w[...])
    heads = pre.shape[1] // HEAD_SIZE
    queries = heads * 2 // 3
    pre[...] = projected[:, : heads * HEAD_SIZE]
    c, s = cos[...], sin[...]
    for h in range(heads):
        cols = slice(h * HEAD_SIZE, (h + 1) * HEAD_SIZE)
        head = projected[:, cols]
        unit = head * rms_scale(head) * (gain_q[...] if h < queries else gain_k[...])
        qkv[:, cols] = (unit * c + pltpu.roll(unit, HEAD_SIZE // 2, 1) * s).astype(bf16)
    qkv[:, heads * HEAD_SIZE :] = projected[:, heads * HEAD_SIZE :].astype(bf16)


def project(x_slots, w, gain, gain_q, gain_k, cos, sin):
    rows, width = x_slots[0].shape
    cols = 1024
    pre_cols = 768
    tile = lambda c: pl.BlockSpec((rows, c), lambda j: (j, 0))
    return call(
        project_kernel,
        (WAYS,),
        [whole(x.shape) for x in x_slots]
        + [whole((width, cols)), whole(gain.shape), whole(gain_q.shape), whole(gain_k.shape)]
        + [tile(HEAD_SIZE), tile(HEAD_SIZE)],
        [((WAYS * rows, width), bf16), ((WAYS * rows, cols), bf16), ((WAYS * rows, pre_cols), f32)],
        [tile(width), tile(cols), tile(pre_cols)],
        [pltpu.VMEM((rows, width), bf16)],
        flops=2 * WAYS * rows * width * cols,
        size=20 << 20,
    )(*x_slots, w, gain, gain_q, gain_k, cos, sin)


def shard_starts(place, size):
    return [pl.multiple_of(lax.rem(place[0] + WAYS - s, WAYS) * size, size) for s in range(WAYS)]


def causal_fill(scores):
    row = lax.broadcasted_iota(jnp.int32, scores.shape, 0)
    col = lax.broadcasted_iota(jnp.int32, scores.shape, 1)
    return jnp.where(col <= row, scores, -1e30)


def attend_kernel(place, q, k, v, ctx, lse):
    size = q.shape[0] // WAYS
    starts = shard_starts(place, size)
    for s in range(WAYS):
        rows = pl.ds(starts[s], size)
        for g in range(q.shape[1] // HEAD_SIZE):
            cols = slice(g * HEAD_SIZE, (g + 1) * HEAD_SIZE)
            query = q[rows, cols]
            blocks = []
            for t in range(s + 1):
                scores = nt(query, k[pl.ds(starts[t], size), :])
                blocks.append(causal_fill(scores) if t == s else scores)
            top = functools.reduce(
                jnp.maximum, [jnp.max(b, axis=-1, keepdims=True) for b in blocks]
            )
            raised = [jnp.exp((b - top) * score_scale) for b in blocks]
            summed = functools.reduce(
                jnp.add, [jnp.sum(b, axis=-1, keepdims=True) for b in raised]
            )
            inverse = 1.0 / summed
            out = functools.reduce(
                jnp.add,
                [
                    nn((b * inverse).astype(bf16), v[pl.ds(starts[t], size), :])
                    for t, b in enumerate(raised)
                ],
            )
            ctx[rows, cols] = out.astype(bf16)
            lse[rows, g : g + 1] = top * score_scale + jnp.log(summed)


def attend(place, qkv):
    rows = qkv.shape[0]
    pairs = 2
    return call(
        attend_kernel,
        (pairs,),
        [
            pl.BlockSpec(memory_space=pltpu.SMEM),
            pl.BlockSpec((rows, 2 * HEAD_SIZE), lambda p: (0, p)),
            pl.BlockSpec((rows, HEAD_SIZE), lambda p: (0, 4 + p)),
            pl.BlockSpec((rows, HEAD_SIZE), lambda p: (0, 6 + p)),
        ],
        [((rows, 4 * HEAD_SIZE), bf16), ((rows, 2 * HEAD_SIZE), f32)],
        [
            pl.BlockSpec((rows, 2 * HEAD_SIZE), lambda p: (0, p)),
            pl.BlockSpec((rows, HEAD_SIZE), lambda p: (0, p)),
        ],
        flops=8 * rows * rows * HEAD_SIZE,
        size=2 << 20,
        exps=2 * rows * rows,
    )(place, qkv, qkv, qkv)


def mix_kernel(own, below, far, above, c0, c1, c2, c3, w, gain, normed, hidden, ctx_rows, acc, c_s):
    k = pl.program_id(0)
    size = own.shape[0]

    @pl.when(k == 0)
    def _():
        for i, ref in enumerate((own, below, far, above)):
            acc[i * size : (i + 1) * size] = ref[...].astype(f32)

    for kk, ref in enumerate((c0, c1, c2, c3)):

        @pl.when(k == kk)
        def _():
            for i in range(WAYS):
                source = (i - kk) % WAYS
                c_s[i * size : (i + 1) * size] = ref[source * size : (source + 1) * size]

    ctx_rows[...] = c_s[:size]
    for i in range(WAYS):
        rows = slice(i * size, (i + 1) * size)
        acc[rows] += nt(c_s[rows], w[...])

    @pl.when(k == WAYS - 1)
    def _():
        hidden[...] = acc[:size]
        for i in range(WAYS):
            rows = slice(i * size, (i + 1) * size)
            h = acc[rows]
            normed[rows] = (h * rms_scale(h) * gain[...]).astype(bf16)


def mix(x_slots, contexts, w_out_full, gain):
    size, width = x_slots[0].shape
    rows, inner = contexts[0].shape
    return call(
        mix_kernel,
        (WAYS,),
        [whole(x.shape) for x in x_slots]
        + [whole(c.shape) for c in contexts]
        + [pl.BlockSpec((width, inner), lambda k: (0, k)), whole(gain.shape)],
        [((rows, width), bf16), ((size, width), f32), ((size, WAYS * inner), bf16)],
        [whole((rows, width)), whole((size, width)), pl.BlockSpec((size, inner), lambda k: (0, k))],
        [pltpu.VMEM((rows, width), f32), pltpu.VMEM((rows, inner), bf16)],
        flops=2 * rows * width * WAYS * inner,
        size=24 << 20,
    )(*x_slots, *contexts, w_out_full, gain)


def feed_kernel(n, w_gate, w_up, out):
    size = 256
    for i in range(n.shape[0] // size):
        rows = slice(i * size, (i + 1) * size)
        gate = nn(n[rows], w_gate[...])
        up = nn(n[rows], w_up[...])
        sig = 1.0 / (1.0 + jnp.exp(-gate))
        silu = gate * sig
        out[0, rows] = (up * sig * (1.0 + gate * (1.0 - sig))).astype(bf16)
        out[1, rows] = silu.astype(bf16)
        out[2, rows] = (silu * up).astype(bf16)


def feed(normed, weights, ff_width):
    rows, width = normed.shape
    tile = 256
    tiles = ff_width // tile
    col = lambda c: pl.BlockSpec((width, tile), lambda j: (0, c * tiles + j))
    return call(
        feed_kernel,
        (tiles,),
        [whole((rows, width)), col(0), col(1)],
        [((3, rows, ff_width), bf16)],
        [pl.BlockSpec((3, rows, tile), lambda j: (0, 0, j))],
        flops=4 * rows * width * ff_width,
        size=26 << 20,
        exps=rows * ff_width,
    )(normed, weights, weights)[0]


def feed_back_kernel(d, w_down, slopes, out):
    size = 256
    for i in range(d.shape[0] // size):
        rows = slice(i * size, (i + 1) * size)
        d_act = nn(d[rows], w_down[...])
        out[0, rows] = (d_act * slopes[0, rows].astype(f32)).astype(bf16)
        out[1, rows] = (d_act * slopes[1, rows].astype(f32)).astype(bf16)


def feed_back(d_branch, w_down, forward):
    rows, width = d_branch.shape
    ff_width = forward.shape[2]
    tile = 256
    return call(
        feed_back_kernel,
        (ff_width // tile,),
        [
            whole((rows, width)),
            pl.BlockSpec((width, tile), lambda j: (0, j)),
            pl.BlockSpec((2, rows, tile), lambda j: (0, 0, j)),
        ],
        [((2, rows, ff_width), bf16)],
        [pl.BlockSpec((2, rows, tile), lambda j: (0, 0, j))],
        flops=2 * rows * width * ff_width,
        size=22 << 20,
    )(d_branch, w_down, forward)[0]


def back_kernel(slots, size, lone, a, b, wa, wb, *outs):
    for slot, out in zip(slots, outs):
        rows = slice(0, size) if lone else slice(slot * size, (slot + 1) * size)
        out[...] = (nt(a[0, rows], wa[...]) + nt(b[0, rows], wb[...])).astype(bf16)


def slot_shapes(slots, size, width, tile):
    return [((size, width), bf16) for _ in slots], [
        pl.BlockSpec((size, tile), lambda n: (0, n)) for _ in slots
    ]


def back_feed(d_all, weights, slots, width, size):
    ff_width = d_all.shape[2]
    tile = 512
    lone = len(slots) == 1
    rows = size if lone else WAYS * size
    row_at = slots[0] if lone else 0
    outs, out_specs = slot_shapes(slots, size, width, tile)
    return call(
        functools.partial(back_kernel, slots, size, lone),
        (width // tile,),
        [
            whole((1, rows, ff_width), (0, row_at, 0)),
            whole((1, rows, ff_width), (1, row_at, 0)),
            pl.BlockSpec((tile, ff_width), lambda n: (n, 0)),
            pl.BlockSpec((tile, ff_width), lambda n: (n, 1)),
        ],
        outs,
        out_specs,
        flops=4 * len(slots) * size * width * ff_width,
        size=20 << 20,
    )(d_all, d_all, weights, weights)


def down_kernel(slots, size, a, wa, *outs):
    for slot, out in zip(slots, outs):
        out[...] = nt(a[0, slot * size : (slot + 1) * size], wa[...]).astype(bf16)


def down(d_all, weights, slots, width, size):
    ff_width = d_all.shape[2]
    tile = 512
    rows = WAYS * size
    outs, out_specs = slot_shapes(slots, size, width, tile)
    return call(
        functools.partial(down_kernel, slots, size),
        (width // tile,),
        [whole((1, rows, ff_width), (2, 0, 0)), pl.BlockSpec((tile, ff_width), lambda n: (n, 0))],
        outs,
        out_specs,
        flops=2 * rows * width * ff_width,
        size=14 << 20,
    )(d_all, weights)


def grads_kernel(n, a, out):
    width = a.shape[2]
    n_tile = n[...]
    for c in range(a.shape[0]):
        out[:, c * width : (c + 1) * width] = tn(n_tile, a[c]).astype(bf16)


def row_grads(left, right, first, count):
    rows, width = left.shape
    cols = right.shape[2]
    tile = 256
    return call(
        grads_kernel,
        (width // tile,),
        [
            pl.BlockSpec((rows, tile), lambda j: (0, j)),
            whole((count, rows, cols), (first // count, 0, 0)),
        ],
        [((width, count * cols), bf16)],
        [pl.BlockSpec((tile, count * cols), lambda j: (j, 0))],
        flops=2 * rows * width * cols * count,
        size=(4 + 9 * count) << 20,
    )(left, right)[0]


def branch_kernel(own, arrived, hidden, cotangent, live, gain, w, d_hidden, d_attended, c0, c1, c2, c3):
    k = pl.program_id(0)

    @pl.when(k == 0)
    def _():
        d_normed = own[...].astype(f32) + arrived[...].astype(f32)
        h = hidden[...]
        total = cotangent[...].astype(f32) * live[...] + norm_back(
            d_normed, h, rms_scale(h), gain[...]
        )
        d_hidden[...] = total
        d_attended[...] = total.astype(bf16)

    value = nn(d_attended[...], w[...]).astype(bf16)
    for kk, ref in enumerate((c0, c1, c2, c3)):

        @pl.when(k == kk)
        def _():
            ref[...] = value


def branch(parts, hidden, cotangent, live, gain, w_out_full, inner):
    size, width = hidden.shape
    return call(
        branch_kernel,
        (WAYS,),
        [whole((size, width))] * 4
        + [whole(live.shape), whole(gain.shape), pl.BlockSpec((width, inner), lambda k: (0, k))],
        [((size, width), f32), ((size, width), bf16)] + [((size, inner), bf16)] * WAYS,
        [whole((size, width))] * 2 + [whole((size, inner))] * WAYS,
        flops=2 * size * width * WAYS * inner,
        size=16 << 20,
    )(*parts, hidden, cotangent, live, gain, w_out_full)


def head_back(d_head, pre_head, gain, c, s):
    d_unit = d_head * c - pltpu.roll(d_head, HEAD_SIZE // 2, 1) * s
    scale = rms_scale(pre_head)
    return norm_back(d_unit, pre_head, scale, gain), jnp.sum(
        d_unit * pre_head * scale, axis=0, keepdims=True
    )


def attend_back_kernel(place, q, k, v, d0, d1, d2, d3, lse, pre_q, pre_k, cos, sin, gain_q, gain_k, dq_out, dk_out, dv_out, sum_q, sum_k, d_s, dk, dv):
    size = q.shape[0] // WAYS
    starts = shard_starts(place, size)
    for slot, ref in enumerate((d0, d1, d2, d3)):
        d_s[slot * size : (slot + 1) * size] = ref[...]
    dk[...] = jnp.zeros_like(dk)
    dv[...] = jnp.zeros_like(dv)
    total_q = jnp.zeros((1, HEAD_SIZE), f32)
    for s in range(WAYS):
        rows = pl.ds(starts[s], size)
        for g in range(q.shape[1] // HEAD_SIZE):
            cols = slice(g * HEAD_SIZE, (g + 1) * HEAD_SIZE)
            query, d_out, log_total = q[rows, cols], d_s[rows, cols], lse[rows, g : g + 1]
            probs, d_probs = [], []
            for t in range(s + 1):
                seen = pl.ds(starts[t], size)
                scores = nt(query, k[seen, :]) * score_scale
                scores = causal_fill(scores) if t == s else scores
                probs.append(jnp.exp(scores - log_total))
                d_probs.append(nt(d_out, v[seen, :]))
            row_dot = functools.reduce(
                jnp.add, [jnp.sum(p * d, axis=-1, keepdims=True) for p, d in zip(probs, d_probs)]
            )
            d_query = jnp.zeros((size, HEAD_SIZE), f32)
            for t in range(s + 1):
                seen = pl.ds(starts[t], size)
                d_scores = (probs[t] * (d_probs[t] - row_dot)).astype(bf16)
                dv[seen, :] += tn(probs[t].astype(bf16), d_out)
                dk[seen, :] += tn(d_scores, query)
                d_query += nn(d_scores, k[seen, :])
            d_pre, part = head_back(
                d_query * score_scale, pre_q[rows, cols], gain_q[...], cos[rows, :], sin[rows, :]
            )
            dq_out[rows, cols] = d_pre.astype(bf16)
            total_q += part
    d_pre, part = head_back(dk[...] * score_scale, pre_k[...], gain_k[...], cos[...], sin[...])
    dk_out[...] = d_pre.astype(bf16)
    dv_out[...] = dv[...].astype(bf16)
    sum_q[...] = jnp.broadcast_to(total_q, sum_q.shape)
    sum_k[...] = jnp.broadcast_to(part, sum_k.shape)


def attend_back(place, qkv, d_slots, lse, pre, cos, sin, gain_q, gain_k):
    rows = qkv.shape[0]
    size = rows // WAYS
    one, two = HEAD_SIZE, 2 * HEAD_SIZE
    cols = lambda r, c, at=0: pl.BlockSpec((r, c), lambda p: (0, at + p))
    return call(
        attend_back_kernel,
        (2,),
        [pl.BlockSpec(memory_space=pltpu.SMEM), cols(rows, two), cols(rows, one, 4), cols(rows, one, 6)]
        + [cols(size, two)] * WAYS
        + [cols(rows, one), cols(rows, two), cols(rows, one, 4)]
        + [whole((rows, one)), whole((rows, one)), whole((1, one)), whole((1, one))],
        [
            ((rows, 2 * two), bf16),
            ((rows, two), bf16),
            ((rows, two), bf16),
            ((8, two), f32),
            ((8, two), f32),
        ],
        [cols(rows, two), cols(rows, one), cols(rows, one), cols(8, one), cols(8, one)],
        [pltpu.VMEM((rows, two), bf16), pltpu.VMEM((rows, one), f32), pltpu.VMEM((rows, one), f32)],
        flops=40 * rows * rows * HEAD_SIZE,
        size=12 << 20,
        exps=4 * rows * rows,
    )(place, qkv, qkv, qkv, *d_slots, lse, pre, pre, cos, sin, gain_q, gain_k)


def back_project_kernel(size, q, k, v, w, *outs):
    for slot, out in zip((1, 2, 3, 0), outs):
        rows = slice(slot * size, (slot + 1) * size)
        total = nt(q[rows], w[:, :512]) + nt(k[rows], w[:, 512:768]) + nt(v[rows], w[:, 768:])
        out[...] = total.astype(bf16)


def back_project(parts, w, width, size):
    tile = 512
    outs, out_specs = slot_shapes((1, 2, 3, 0), size, width, tile)
    return call(
        functools.partial(back_project_kernel, size),
        (width // tile,),
        [whole(p.shape) for p in parts] + [pl.BlockSpec((tile, 1024), lambda n: (n, 0))],
        outs,
        out_specs,
        flops=2 * WAYS * size * width * 1024,
        size=10 << 20,
    )(*parts, w)


def attend_grads_kernel(n, q, k, v, d, c, gains, out):
    n_tile = n[...]
    at = 0
    for ref in (q, k, v):
        wide = ref.shape[1]
        out[:, at : at + wide] = tn(n_tile, ref[...]).astype(bf16)
        at += wide
    out[:, at : at + c.shape[1]] = tn(d[...], c[...]).astype(bf16)
    out[:, at + c.shape[1] :] = gains[...]


def attend_grads(normed, parts, d_attended, ctx_rows, gains):
    rows, width = normed.shape
    tile = 256
    cols = sum(p.shape[1] for p in parts) + ctx_rows.shape[1] + gains.shape[1]
    return call(
        attend_grads_kernel,
        (width // tile,),
        [pl.BlockSpec((rows, tile), lambda j: (0, j))]
        + [whole(p.shape) for p in parts]
        + [
            pl.BlockSpec((d_attended.shape[0], tile), lambda j: (0, j)),
            whole(ctx_rows.shape),
            pl.BlockSpec((tile, gains.shape[1]), lambda j: (j, 0)),
        ],
        [((width, cols), bf16)],
        [pl.BlockSpec((tile, cols), lambda j: (j, 0))],
        flops=2 * rows * width * 1536,
        size=20 << 20,
    )(normed, *parts, d_attended, ctx_rows, gains)[0]


def local(
    tokens,
    norm_attn,
    w_query,
    key_matrix,
    value_matrix,
    gain_query,
    gain_key,
    w_output,
    norm_ffn,
    w_gate,
    w_up,
    w_down,
    cotangent,
    lengths,
    deal_order,
):
    place = lax.axis_index("tensor")
    data_ways = lax.axis_size("dp")
    size, width = tokens.shape
    shard_rows = norm_attn.shape[0]
    gain_rows = gain_query.shape[0]
    q_width = w_query.shape[1]
    kv_width = key_matrix.shape[1]
    qkv_width = q_width + 2 * kv_width
    ff_width = w_gate.shape[1]
    place_ref = place.reshape(1).astype(jnp.int32)

    x1 = hop(tokens)
    x2 = hop(x1)
    x3 = hop(x2)
    seq_len = sequence_length(lengths, deal_order, lax.axis_index("dp"))
    offsets = jnp.arange(size, dtype=jnp.int32)
    own_live = (place * size + offsets < seq_len).astype(f32)[:, None]
    x3, d_branch, w_out = together(x3, (cotangent.astype(f32) * own_live).astype(bf16), w_output.T)
    x_slots = [tokens, x1, x2, x3]
    d1 = hop(d_branch)
    w1 = hop(w_out)
    w2 = hop(w1)
    w3 = hop(w2)

    column = lambda v: jnp.pad(v, (0, shard_rows - v.shape[0]))[:, None]
    attn_part = jnp.concatenate(
        [w_query, key_matrix, value_matrix]
        + [column(v) for v in (norm_attn, norm_ffn, gain_query, gain_key)]
        + [jnp.zeros((shard_rows, 124), bf16)],
        axis=1,
    )
    attn_full = lax.all_gather(attn_part, "dp", axis=0, tiled=True)
    gain_block = attn_full[:, qkv_width : qkv_width + 4].astype(f32)
    norm_attn_all = gain_block[:, 0].reshape(1, width)
    norm_ffn_all = gain_block[:, 1].reshape(1, width)
    by_shard = gain_block.reshape(data_ways, shard_rows, 4)[:, :gain_rows]
    gain_q = by_shard[:, :, 2].reshape(1, HEAD_SIZE)
    gain_k = by_shard[:, :, 3].reshape(1, HEAD_SIZE)

    gate_up_full = lax.all_gather(
        jnp.concatenate([w_gate, w_up], axis=1), "dp", axis=0, tiled=True
    )
    w_out_full = lax.all_gather(
        jnp.concatenate([w_out, w1, w2, w3], axis=1), "dp", axis=0, tiled=True
    )
    down_full = lax.all_gather(w_down.T, "dp", axis=0, tiled=True)

    position = jnp.concatenate([((place - j) % WAYS) * size + offsets for j in range(WAYS)])
    cos, sin = rope_tables(position)

    normed_attn, qkv, pre = project(x_slots, attn_full, norm_attn_all, gain_q, gain_k, cos, sin)
    context, log_total = attend(place_ref, qkv)
    context, d1 = together(context, d1)
    c1 = hop(context)
    c2 = hop(c1)
    c3, d1 = together(hop(c2), d1)
    d2 = hop(d1)
    normed_ffn, hidden, ctx_rows = mix(x_slots, [context, c1, c2, c3], w_out_full, norm_ffn_all)

    normed_ffn, d2 = together(normed_ffn, d2)
    d3 = hop(d2)
    forward = feed(normed_ffn, gate_up_full, ff_width)
    d_branch_all = jnp.concatenate([d_branch, d1, d2, d3], axis=0)
    grads_down = row_grads(d_branch_all, forward, 2, 1)
    forward, grads_down = together(forward, grads_down)
    grads_down = lax.psum_scatter(grads_down, "dp", scatter_dimension=0, tiled=True)
    d_all = feed_back(d_branch_all, down_full, forward)
    (b1,) = back_feed(d_all, gate_up_full, (1,), width, size)
    b_sum = hop(b1)
    b2, b3, b0 = back_feed(d_all, gate_up_full, (2, 3, 0), width, size)
    b_sum, d_all = together(add(b2, b_sum), d_all)
    b_sum = hop(b_sum)
    grads_feed = row_grads(normed_ffn, d_all, 0, 2)
    b_sum, grads_feed, forward = together(add(b3, b_sum), grads_feed, forward)
    b_sum = hop(b_sum)
    y1, y2, y3, y0 = down(forward, down_full, (1, 2, 3, 0), width, size)
    b_sum, y1, y2, y3, y0 = together(b_sum, y1, y2, y3, y0)
    grads_feed, grads_down = together(grads_feed, grads_down)
    grads_feed = lax.psum_scatter(grads_feed, "dp", scatter_dimension=0, tiled=True)

    d_hidden, d_attended, p0, p1, p2, p3 = branch(
        (b0, b_sum), hidden, cotangent, own_live, norm_ffn_all, w_out_full, q_width
    )
    s1, s2, s3, y1 = together(shift_by(p3, 1), shift_by(p2, 2), shift_by(p1, -1), y1)
    y_sum = hop(y1)
    d_q, d_k, d_v, sum_q, sum_k = attend_back(
        place_ref, qkv, [p0, s1, s2, s3], log_total, pre, cos, sin, gain_q, gain_k
    )
    d_q, y_sum = together(d_q, y_sum)
    parts = (d_q, d_k, d_v)
    e1, e2, e3, e0 = back_project(parts, attn_full, width, size)
    e_sum, d_q = together(e1, d_q)
    parts = (d_q, d_k, d_v)
    e_sum = hop(e_sum)
    spread = lambda v: jnp.pad(
        v.reshape(data_ways, gain_rows), ((0, 0), (0, shard_rows - gain_rows))
    ).reshape(-1, 1)
    gains = jnp.concatenate(
        [
            spread(sum_q[0, :HEAD_SIZE] + sum_q[0, HEAD_SIZE:]),
            spread(sum_k[0, :HEAD_SIZE] + sum_k[0, HEAD_SIZE:]),
            jnp.zeros((width, 126), f32),
        ],
        axis=1,
    ).astype(bf16)
    grads_attn = attend_grads(normed_attn, parts, d_attended, ctx_rows, gains)
    grads_attn, grads_feed, e_sum = together(grads_attn, grads_feed, e_sum)
    grads_attn = lax.psum_scatter(grads_attn, "dp", scatter_dimension=0, tiled=True)
    e_sum = hop(add(e2, e_sum))
    e_sum, y_sum = together(hop(add(e3, e_sum)), y_sum)
    d_normed_attn = e0.astype(f32) + e_sum.astype(f32)

    y_sum = hop(add(y2, y_sum))
    y_sum = hop(add(y3, y_sum))
    ffn_out = y0.astype(f32) + y_sum.astype(f32)
    block_out = ((hidden + ffn_out) * own_live).astype(bf16)
    own_tokens = tokens.astype(f32)
    d_tokens = d_hidden + norm_back(d_normed_attn, own_tokens, rms_scale(own_tokens), norm_attn_all)

    grads_feed = grads_feed.astype(f32)
    grad_gate, grad_up = grads_feed[:, :ff_width], grads_feed[:, ff_width:]
    grad_down = grads_down.astype(f32).T
    grad_qkv = grads_attn[:, :qkv_width].astype(f32)
    grad_query = grad_qkv[:, :q_width]
    grad_key = grad_qkv[:, q_width : q_width + kv_width]
    grad_value = grad_qkv[:, q_width + kv_width :]
    g0, g1, g2, g3 = [
        grads_attn[:, qkv_width + k * q_width : qkv_width + (k + 1) * q_width] for k in range(WAYS)
    ]
    grad_output = (
        g0.astype(f32)
        + shift_by(g1, -1).astype(f32)
        + shift_by(g2, 2).astype(f32)
        + shift_by(g3, 1).astype(f32)
    ).T
    gain_sums = grads_attn[:gain_rows, qkv_width + WAYS * q_width :].astype(f32)
    own_attn = jnp.sum(
        attn_part[:, :qkv_width].astype(f32) * grad_qkv, axis=1
    ) / norm_attn.astype(f32)
    own_ffn = jnp.sum(
        w_gate.astype(f32) * grad_gate + w_up.astype(f32) * grad_up, axis=1
    ) / norm_ffn.astype(f32)
    small = jnp.concatenate([own_attn, own_ffn, gain_sums[:, 0], gain_sums[:, 1]])
    small = small + shift_by(small, 1)
    small = small + shift_by(small, 2)
    grad_norm_attn = small[:shard_rows]
    grad_norm_ffn = small[shard_rows : 2 * shard_rows]
    grad_gain_query = small[2 * shard_rows : 2 * shard_rows + gain_rows]
    grad_gain_key = small[2 * shard_rows + gain_rows :]
    return (
        block_out,
        d_tokens.astype(bf16),
        grad_norm_attn,
        grad_query,
        grad_key,
        grad_value,
        grad_gain_query,
        grad_gain_key,
        grad_output,
        grad_norm_ffn,
        grad_gate,
        grad_up,
        grad_down,
    )


def solution(mesh):
    return jax.shard_map(
        local,
        mesh=mesh,
        in_specs=(
            P(("dp", "tensor"), None),
            P("dp"),
            P("dp", "tensor"),
            P("dp", "tensor"),
            P("dp", "tensor"),
            P("dp"),
            P("dp"),
            P("tensor", "dp"),
            P("dp"),
            P("dp", "tensor"),
            P("dp", "tensor"),
            P("tensor", "dp"),
            P(("dp", "tensor"), None),
            P(),
            P(),
        ),
        out_specs=(
            P(("dp", "tensor"), None),
            P(("dp", "tensor"), None),
            P("dp"),
            P("dp", "tensor"),
            P("dp", "tensor"),
            P("dp", "tensor"),
            P("dp"),
            P("dp"),
            P("tensor", "dp"),
            P("dp"),
            P("dp", "tensor"),
            P("dp", "tensor"),
            P("tensor", "dp"),
        ),
        check_vma=False,
    )
```

```python
import functools

import jax
import jax.numpy as jnp
from jax import lax
from jax.experimental import pallas as pl
from jax.experimental.pallas import tpu as pltpu
from jax.sharding import PartitionSpec as P

QUERY_HEADS = 16
KEY_VALUE_HEADS = 8
HEAD_SIZE = 128

norm_eps = 1e-06
rope_base = 1000000.0
score_scale = HEAD_SIZE ** (-0.5)
f32 = jnp.float32
bf16 = jnp.bfloat16
WAYS = 4
ROOM = 58 << 20


def nn(left, right):
    return lax.dot_general(left, right, (((1,), (0,)), ((), ())), preferred_element_type=f32)


def nt(left, right):
    return lax.dot_general(left, right, (((1,), (1,)), ((), ())), preferred_element_type=f32)


def tn(left, right):
    return lax.dot_general(left, right, (((0,), (0,)), ((), ())), preferred_element_type=f32)


def rms_scale(value_vectors):
    return lax.rsqrt(jnp.mean(value_vectors * value_vectors, axis=-1, keepdims=True) + norm_eps)


def norm_back(d_unit, pre_values, pre_scale, gain_values):
    mixed_terms = gain_values * d_unit
    return pre_scale * mixed_terms - pre_values * pre_scale**3 * jnp.mean(
        mixed_terms * pre_values, axis=-1, keepdims=True
    )


def rope_tables(position):
    half_dim = HEAD_SIZE // 2
    inverse_freq = rope_base ** (-2.0 * jnp.arange(half_dim, dtype=f32) / HEAD_SIZE)
    angles = position.astype(f32)[:, None] * inverse_freq[None, :]
    cosine, sine = jnp.cos(angles), jnp.sin(angles)
    return jnp.concatenate([cosine, cosine], axis=1), jnp.concatenate([-sine, sine], axis=1)


def sequence_length(lengths, deal_order, group_id):
    slots = jnp.arange(deal_order.shape[0], dtype=jnp.int32)
    seq_taken = jnp.sum(jnp.where(slots == group_id, deal_order, 0))
    return jnp.sum(jnp.where(slots == seq_taken, lengths, 0))


def shift_by(value, step):
    return lax.ppermute(value, "tensor", [(i, (i + step) % WAYS) for i in range(WAYS)])


def hop(value):
    return shift_by(value, 1)


def together(*values):
    return lax.optimization_barrier(values)


def add(block, arrived):
    return (block.astype(f32) + arrived.astype(f32)).astype(bf16)


def whole(shape, index=None):
    rank = len(shape)
    place = index if index is not None else (0,) * rank
    return pl.BlockSpec(shape, lambda *_: place, pipeline_mode=pl.Buffered(1))


def call(kernel, grid, in_specs, outs, out_specs, scratch=(), flops=0, size=0, exps=0):
    return pl.pallas_call(
        kernel,
        grid=grid,
        in_specs=in_specs,
        out_shape=[jax.ShapeDtypeStruct(s, d) for s, d in outs],
        out_specs=out_specs,
        scratch_shapes=list(scratch),
        compiler_params=pltpu.CompilerParams(vmem_limit_bytes=ROOM),
        cost_estimate=pl.CostEstimate(flops=flops, bytes_accessed=size, transcendentals=exps),
    )


def pick_slot(step, slots, x_s):
    for j, ref in enumerate(slots):

        @pl.when(step == j)
        def _():
            x_s[...] = ref[...]


def project_kernel(own, below, far, above, w, gain, gain_q, gain_k, cos, sin, normed, qkv, pre, x_s):
    pick_slot(pl.program_id(0), (own, below, far, above), x_s)
    x = x_s[...].astype(f32)
    n = (x * rms_scale(x) * gain[...]).astype(bf16)
    normed[...] = n
    projected = nn(n, w[...])
    heads = pre.shape[1] // HEAD_SIZE
    queries = heads * 2 // 3
    pre[...] = projected[:, : heads * HEAD_SIZE]
    c, s = cos[...], sin[...]
    for h in range(heads):
        cols = slice(h * HEAD_SIZE, (h + 1) * HEAD_SIZE)
        head = projected[:, cols]
        unit = head * rms_scale(head) * (gain_q[...] if h < queries else gain_k[...])
        qkv[:, cols] = (unit * c + pltpu.roll(unit, HEAD_SIZE // 2, 1) * s).astype(bf16)
    qkv[:, heads * HEAD_SIZE :] = projected[:, heads * HEAD_SIZE :].astype(bf16)


def project(x_slots, w, gain, gain_q, gain_k, cos, sin):
    rows, width = x_slots[0].shape
    cols = 1024
    pre_cols = 768
    tile = lambda c: pl.BlockSpec((rows, c), lambda j: (j, 0))
    return call(
        project_kernel,
        (WAYS,),
        [whole(x.shape) for x in x_slots]
        + [whole((width, cols)), whole(gain.shape), whole(gain_q.shape), whole(gain_k.shape)]
        + [tile(HEAD_SIZE), tile(HEAD_SIZE)],
        [((WAYS * rows, width), bf16), ((WAYS * rows, cols), bf16), ((WAYS * rows, pre_cols), f32)],
        [tile(width), tile(cols), tile(pre_cols)],
        [pltpu.VMEM((rows, width), bf16)],
        flops=2 * WAYS * rows * width * cols,
        size=20 << 20,
    )(*x_slots, w, gain, gain_q, gain_k, cos, sin)


def shard_starts(place, size):
    return [pl.multiple_of(lax.rem(place[0] + WAYS - s, WAYS) * size, size) for s in range(WAYS)]


def causal_fill(scores):
    row = lax.broadcasted_iota(jnp.int32, scores.shape, 0)
    col = lax.broadcasted_iota(jnp.int32, scores.shape, 1)
    return jnp.where(col <= row, scores, -1e30)


def attend_kernel(place, q, k, v, ctx, lse):
    size = q.shape[0] // WAYS
    starts = shard_starts(place, size)
    for s in range(WAYS):
        rows = pl.ds(starts[s], size)
        for g in range(q.shape[1] // HEAD_SIZE):
            cols = slice(g * HEAD_SIZE, (g + 1) * HEAD_SIZE)
            query = q[rows, cols]
            blocks = []
            for t in range(s + 1):
                scores = nt(query, k[pl.ds(starts[t], size), :])
                blocks.append(causal_fill(scores) if t == s else scores)
            top = functools.reduce(
                jnp.maximum, [jnp.max(b, axis=-1, keepdims=True) for b in blocks]
            )
            raised = [jnp.exp((b - top) * score_scale) for b in blocks]
            summed = functools.reduce(
                jnp.add, [jnp.sum(b, axis=-1, keepdims=True) for b in raised]
            )
            inverse = 1.0 / summed
            out = functools.reduce(
                jnp.add,
                [
                    nn((b * inverse).astype(bf16), v[pl.ds(starts[t], size), :])
                    for t, b in enumerate(raised)
                ],
            )
            ctx[rows, cols] = out.astype(bf16)
            lse[rows, g : g + 1] = top * score_scale + jnp.log(summed)


def attend(place, qkv):
    rows = qkv.shape[0]
    pairs = 2
    return call(
        attend_kernel,
        (pairs,),
        [
            pl.BlockSpec(memory_space=pltpu.SMEM),
            pl.BlockSpec((rows, 2 * HEAD_SIZE), lambda p: (0, p)),
            pl.BlockSpec((rows, HEAD_SIZE), lambda p: (0, 4 + p)),
            pl.BlockSpec((rows, HEAD_SIZE), lambda p: (0, 6 + p)),
        ],
        [((rows, 4 * HEAD_SIZE), bf16), ((rows, 2 * HEAD_SIZE), f32)],
        [
            pl.BlockSpec((rows, 2 * HEAD_SIZE), lambda p: (0, p)),
            pl.BlockSpec((rows, HEAD_SIZE), lambda p: (0, p)),
        ],
        flops=8 * rows * rows * HEAD_SIZE,
        size=2 << 20,
        exps=2 * rows * rows,
    )(place, qkv, qkv, qkv)


def mix_kernel(own, below, far, above, c0, c1, c2, c3, wa, wb, gain, normed, hidden, ctx_rows, x_s, c_s):
    i = pl.program_id(0)
    size = own.shape[0]
    inner = c0.shape[1]
    pick_slot(i, (own, below, far, above), x_s)
    for k, ref in enumerate((c0, c1, c2, c3)):
        start = pl.multiple_of(lax.rem(i + WAYS - k, WAYS) * size, size)
        c_s[:, k * inner : (k + 1) * inner] = ref[pl.ds(start, size), :]
    wide = wa.shape[1]
    h = x_s[...].astype(f32) + nt(c_s[:, :wide], wa[...]) + nt(c_s[:, wide:], wb[...])
    normed[...] = (h * rms_scale(h) * gain[...]).astype(bf16)

    @pl.when(i == 0)
    def _():
        hidden[...] = h
        ctx_rows[...] = c_s[...]


def mix(x_slots, contexts, weights, gain):
    size, width = x_slots[0].shape
    rows, inner = contexts[0].shape
    cols = WAYS * inner
    return call(
        mix_kernel,
        (WAYS,),
        [whole(x.shape) for x in x_slots]
        + [whole(c.shape) for c in contexts]
        + [whole((width, cols // 2), (0, 3)), whole((width, cols // 2), (0, 4)), whole(gain.shape)],
        [((rows, width), bf16), ((size, width), f32), ((size, cols), bf16)],
        [pl.BlockSpec((size, width), lambda i: (i, 0)), whole((size, width)), whole((size, cols))],
        [pltpu.VMEM((size, width), bf16), pltpu.VMEM((size, cols), bf16)],
        flops=2 * rows * width * cols,
        size=24 << 20,
    )(*x_slots, *contexts, weights, weights, gain)


def feed_kernel(n, w_gate, w_up, out):
    size = 256
    for i in range(n.shape[0] // size):
        rows = slice(i * size, (i + 1) * size)
        gate = nn(n[rows], w_gate[...])
        up = nn(n[rows], w_up[...])
        sig = 1.0 / (1.0 + jnp.exp(-gate))
        silu = gate * sig
        out[0, rows] = (up * sig * (1.0 + gate * (1.0 - sig))).astype(bf16)
        out[1, rows] = silu.astype(bf16)
        out[2, rows] = (silu * up).astype(bf16)


def feed(normed, weights, ff_width):
    rows, width = normed.shape
    tile = 256
    tiles = ff_width // tile
    col = lambda c: pl.BlockSpec((width, tile), lambda j: (0, c * tiles + j))
    return call(
        feed_kernel,
        (tiles,),
        [whole((rows, width)), col(0), col(1)],
        [((3, rows, ff_width), bf16)],
        [pl.BlockSpec((3, rows, tile), lambda j: (0, 0, j))],
        flops=4 * rows * width * ff_width,
        size=26 << 20,
        exps=rows * ff_width,
    )(normed, weights, weights)[0]


def feed_back_kernel(d, w_down, slopes, out):
    size = 256
    for i in range(d.shape[0] // size):
        rows = slice(i * size, (i + 1) * size)
        d_act = nn(d[rows], w_down[...])
        out[0, rows] = (d_act * slopes[0, rows].astype(f32)).astype(bf16)
        out[1, rows] = (d_act * slopes[1, rows].astype(f32)).astype(bf16)


def feed_back(d_branch, w_down, forward):
    rows, width = d_branch.shape
    ff_width = forward.shape[2]
    tile = 256
    return call(
        feed_back_kernel,
        (ff_width // tile,),
        [
            whole((rows, width)),
            pl.BlockSpec((width, tile), lambda j: (0, j)),
            pl.BlockSpec((2, rows, tile), lambda j: (0, 0, j)),
        ],
        [((2, rows, ff_width), bf16)],
        [pl.BlockSpec((2, rows, tile), lambda j: (0, 0, j))],
        flops=2 * rows * width * ff_width,
        size=22 << 20,
    )(d_branch, w_down, forward)[0]


def back_kernel(slots, size, lone, a, b, wa, wb, *outs):
    for slot, out in zip(slots, outs):
        rows = slice(0, size) if lone else slice(slot * size, (slot + 1) * size)
        out[...] = (nt(a[0, rows], wa[...]) + nt(b[0, rows], wb[...])).astype(bf16)


def slot_shapes(slots, size, width, tile):
    return [((size, width), bf16) for _ in slots], [
        pl.BlockSpec((size, tile), lambda n: (0, n)) for _ in slots
    ]


def back_feed(d_all, weights, slots, width, size):
    ff_width = d_all.shape[2]
    tile = 512
    lone = len(slots) == 1
    rows = size if lone else WAYS * size
    row_at = slots[0] if lone else 0
    outs, out_specs = slot_shapes(slots, size, width, tile)
    return call(
        functools.partial(back_kernel, slots, size, lone),
        (width // tile,),
        [
            whole((1, rows, ff_width), (0, row_at, 0)),
            whole((1, rows, ff_width), (1, row_at, 0)),
            pl.BlockSpec((tile, ff_width), lambda n: (n, 0)),
            pl.BlockSpec((tile, ff_width), lambda n: (n, 1)),
        ],
        outs,
        out_specs,
        flops=4 * len(slots) * size * width * ff_width,
        size=20 << 20,
    )(d_all, d_all, weights, weights)


def down_kernel(slots, size, a, wa, *outs):
    for slot, out in zip(slots, outs):
        out[...] = nt(a[0, slot * size : (slot + 1) * size], wa[...]).astype(bf16)


def down(d_all, weights, slots, width, size):
    ff_width = d_all.shape[2]
    tile = 512
    rows = WAYS * size
    outs, out_specs = slot_shapes(slots, size, width, tile)
    return call(
        functools.partial(down_kernel, slots, size),
        (width // tile,),
        [whole((1, rows, ff_width), (2, 0, 0)), pl.BlockSpec((tile, ff_width), lambda n: (n, 0))],
        outs,
        out_specs,
        flops=2 * rows * width * ff_width,
        size=14 << 20,
    )(d_all, weights)


def grads_kernel(n, a, out):
    width = a.shape[2]
    n_tile = n[...]
    for c in range(a.shape[0]):
        out[:, c * width : (c + 1) * width] = tn(n_tile, a[c]).astype(bf16)


def row_grads(left, right, first, count):
    rows, width = left.shape
    cols = right.shape[2]
    tile = 512
    return call(
        grads_kernel,
        (width // tile,),
        [
            pl.BlockSpec((rows, tile), lambda j: (0, j)),
            whole((count, rows, cols), (first // count, 0, 0)),
        ],
        [((width, count * cols), bf16)],
        [pl.BlockSpec((tile, count * cols), lambda j: (j, 0))],
        flops=2 * rows * width * cols * count,
        size=(4 + 9 * count) << 20,
    )(left, right)[0]


def branch_kernel(own, arrived, hidden, cotangent, live, gain, w, d_hidden, d_attended, c0, c1, c2, c3):
    k = pl.program_id(0)

    @pl.when(k == 0)
    def _():
        d_normed = own[...].astype(f32) + arrived[...].astype(f32)
        h = hidden[...]
        total = cotangent[...].astype(f32) * live[...] + norm_back(
            d_normed, h, rms_scale(h), gain[...]
        )
        d_hidden[...] = total
        d_attended[...] = total.astype(bf16)

    value = nn(d_attended[...], w[...]).astype(bf16)
    for kk, ref in enumerate((c0, c1, c2, c3)):

        @pl.when(k == kk)
        def _():
            ref[...] = value


def branch(parts, hidden, cotangent, live, gain, rest_full, inner):
    size, width = hidden.shape
    return call(
        branch_kernel,
        (WAYS,),
        [whole((size, width))] * 4
        + [whole(live.shape), whole(gain.shape), pl.BlockSpec((width, inner), lambda k: (0, 6 + k))],
        [((size, width), f32), ((size, width), bf16)] + [((size, inner), bf16)] * WAYS,
        [whole((size, width))] * 2 + [whole((size, inner))] * WAYS,
        flops=2 * size * width * WAYS * inner,
        size=16 << 20,
    )(*parts, hidden, cotangent, live, gain, rest_full)


def head_back(d_head, pre_head, gain, c, s):
    d_unit = d_head * c - pltpu.roll(d_head, HEAD_SIZE // 2, 1) * s
    scale = rms_scale(pre_head)
    return norm_back(d_unit, pre_head, scale, gain), jnp.sum(
        d_unit * pre_head * scale, axis=0, keepdims=True
    )


def attend_back_kernel(place, q, k, v, d0, d1, d2, d3, lse, pre_q, pre_k, cos, sin, gain_q, gain_k, dq_out, dk_out, dv_out, sum_q, sum_k, d_s, dk, dv):
    size = q.shape[0] // WAYS
    starts = shard_starts(place, size)
    for slot, ref in enumerate((d0, d1, d2, d3)):
        d_s[slot * size : (slot + 1) * size] = ref[...]
    dk[...] = jnp.zeros_like(dk)
    dv[...] = jnp.zeros_like(dv)
    total_q = jnp.zeros((1, HEAD_SIZE), f32)
    for s in range(WAYS):
        rows = pl.ds(starts[s], size)
        for g in range(q.shape[1] // HEAD_SIZE):
            cols = slice(g * HEAD_SIZE, (g + 1) * HEAD_SIZE)
            query, d_out, log_total = q[rows, cols], d_s[rows, cols], lse[rows, g : g + 1]
            probs, d_probs = [], []
            for t in range(s + 1):
                seen = pl.ds(starts[t], size)
                scores = nt(query, k[seen, :]) * score_scale
                scores = causal_fill(scores) if t == s else scores
                probs.append(jnp.exp(scores - log_total))
                d_probs.append(nt(d_out, v[seen, :]))
            row_dot = functools.reduce(
                jnp.add, [jnp.sum(p * d, axis=-1, keepdims=True) for p, d in zip(probs, d_probs)]
            )
            d_query = jnp.zeros((size, HEAD_SIZE), f32)
            for t in range(s + 1):
                seen = pl.ds(starts[t], size)
                d_scores = (probs[t] * (d_probs[t] - row_dot)).astype(bf16)
                dv[seen, :] += tn(probs[t].astype(bf16), d_out)
                dk[seen, :] += tn(d_scores, query)
                d_query += nn(d_scores, k[seen, :])
            d_pre, part = head_back(
                d_query * score_scale, pre_q[rows, cols], gain_q[...], cos[rows, :], sin[rows, :]
            )
            dq_out[rows, cols] = d_pre.astype(bf16)
            total_q += part
    d_pre, part = head_back(dk[...] * score_scale, pre_k[...], gain_k[...], cos[...], sin[...])
    dk_out[...] = d_pre.astype(bf16)
    dv_out[...] = dv[...].astype(bf16)
    sum_q[...] = jnp.broadcast_to(total_q, sum_q.shape)
    sum_k[...] = jnp.broadcast_to(part, sum_k.shape)


def attend_back(place, qkv, d_slots, lse, pre, cos, sin, gain_q, gain_k):
    rows = qkv.shape[0]
    size = rows // WAYS
    one, two = HEAD_SIZE, 2 * HEAD_SIZE
    cols = lambda r, c, at=0: pl.BlockSpec((r, c), lambda p: (0, at + p))
    return call(
        attend_back_kernel,
        (2,),
        [pl.BlockSpec(memory_space=pltpu.SMEM), cols(rows, two), cols(rows, one, 4), cols(rows, one, 6)]
        + [cols(size, two)] * WAYS
        + [cols(rows, one), cols(rows, two), cols(rows, one, 4)]
        + [whole((rows, one)), whole((rows, one)), whole((1, one)), whole((1, one))],
        [
            ((rows, 2 * two), bf16),
            ((rows, two), bf16),
            ((rows, two), bf16),
            ((8, two), f32),
            ((8, two), f32),
        ],
        [cols(rows, two), cols(rows, one), cols(rows, one), cols(8, one), cols(8, one)],
        [pltpu.VMEM((rows, two), bf16), pltpu.VMEM((rows, one), f32), pltpu.VMEM((rows, one), f32)],
        flops=40 * rows * rows * HEAD_SIZE,
        size=12 << 20,
        exps=4 * rows * rows,
    )(place, qkv, qkv, qkv, *d_slots, lse, pre, pre, cos, sin, gain_q, gain_k)


def back_project_kernel(size, q, k, v, w, *outs):
    for slot, out in zip((1, 2, 3, 0), outs):
        rows = slice(slot * size, (slot + 1) * size)
        total = nt(q[rows], w[:, :512]) + nt(k[rows], w[:, 512:768]) + nt(v[rows], w[:, 768:])
        out[...] = total.astype(bf16)


def back_project(parts, w, width, size):
    tile = 512
    outs, out_specs = slot_shapes((1, 2, 3, 0), size, width, tile)
    return call(
        functools.partial(back_project_kernel, size),
        (width // tile,),
        [whole(p.shape) for p in parts] + [pl.BlockSpec((tile, 1024), lambda n: (n, 0))],
        outs,
        out_specs,
        flops=2 * WAYS * size * width * 1024,
        size=10 << 20,
    )(*parts, w)


def attend_grads_kernel(n, q, k, v, w, out, gain_part):
    n_tile = n[...]
    at = 0
    total = jnp.zeros(gain_part.shape, f32)
    for ref in (q, k, v):
        cols = slice(at, at + ref.shape[1])
        product = tn(n_tile, ref[...])
        out[:, cols] = product.astype(bf16)
        total += jnp.sum(product * w[:, cols].astype(f32), axis=1, keepdims=True)
        at += ref.shape[1]
    gain_part[...] = total


def attend_grads(normed, parts, w):
    rows, width = normed.shape
    tile = 512
    cols = sum(p.shape[1] for p in parts)
    return call(
        attend_grads_kernel,
        (width // tile,),
        [pl.BlockSpec((rows, tile), lambda j: (0, j))]
        + [whole(p.shape) for p in parts]
        + [pl.BlockSpec((tile, cols), lambda j: (j, 0))],
        [((width, cols), bf16), ((width, 128), f32)],
        [pl.BlockSpec((tile, cols), lambda j: (j, 0)), pl.BlockSpec((tile, 128), lambda j: (j, 0))],
        flops=2 * rows * width * 1024,
        size=16 << 20,
    )(normed, *parts, w)


def local(
    tokens,
    norm_attn,
    w_query,
    key_matrix,
    value_matrix,
    gain_query,
    gain_key,
    w_output,
    norm_ffn,
    w_gate,
    w_up,
    w_down,
    cotangent,
    lengths,
    deal_order,
):
    place = lax.axis_index("tensor")
    data_ways = lax.axis_size("dp")
    size, width = tokens.shape
    shard_rows = norm_attn.shape[0]
    gain_rows = gain_query.shape[0]
    q_width = w_query.shape[1]
    kv_width = key_matrix.shape[1]
    qkv_width = q_width + 2 * kv_width
    ff_width = w_gate.shape[1]
    place_ref = place.reshape(1).astype(jnp.int32)

    w_out = w_output.T
    x1, w1 = together(hop(tokens), hop(w_out))
    offsets = jnp.arange(size, dtype=jnp.int32)
    position = jnp.concatenate([((place - j) % WAYS) * size + offsets for j in range(WAYS)])
    cos, sin = rope_tables(position)
    seq_len = sequence_length(lengths, deal_order, lax.axis_index("dp"))
    own_live = (position[:size] < seq_len).astype(f32)[:, None]
    d_branch = (cotangent.astype(f32) * own_live).astype(bf16)
    x2, w2, cos, sin, d_branch = together(hop(x1), hop(w1), cos, sin, d_branch)
    w3 = hop(w2)
    x3, d_branch = together(hop(x2), d_branch)
    x_slots = [tokens, x1, x2, x3]
    d1 = hop(d_branch)

    column = lambda v: jnp.pad(v, (0, shard_rows - v.shape[0]))[:, None]
    attn_part = jnp.concatenate(
        [w_query, key_matrix, value_matrix]
        + [column(v) for v in (norm_attn, norm_ffn, gain_query, gain_key)]
        + [jnp.zeros((shard_rows, 124), bf16)],
        axis=1,
    )
    attn_full = lax.all_gather(attn_part, "dp", axis=0, tiled=True)
    gain_block = attn_full[:, qkv_width : qkv_width + 4].astype(f32)
    norm_attn_all = gain_block[:, 0].reshape(1, width)
    norm_ffn_all = gain_block[:, 1].reshape(1, width)
    by_shard = gain_block.reshape(data_ways, shard_rows, 4)[:, :gain_rows]
    gain_q = by_shard[:, :, 2].reshape(1, HEAD_SIZE)
    gain_k = by_shard[:, :, 3].reshape(1, HEAD_SIZE)

    rest_full = lax.all_gather(
        jnp.concatenate([w_gate, w_up, w_out, w1, w2, w3], axis=1), "dp", axis=0, tiled=True
    )
    w_down_part, x2 = together(w_down.T, x2)
    x_slots = [tokens, x1, x2, x3]
    down_full = lax.all_gather(w_down_part, "dp", axis=0, tiled=True)

    normed_attn, qkv, pre = project(x_slots, attn_full, norm_attn_all, gain_q, gain_k, cos, sin)
    context, log_total = attend(place_ref, qkv)
    context, d1 = together(context, d1)
    c1 = hop(context)
    c2 = hop(c1)
    c3, d1 = together(hop(c2), d1)
    d2 = hop(d1)
    normed_ffn, hidden, ctx_rows = mix(x_slots, [context, c1, c2, c3], rest_full, norm_ffn_all)

    normed_ffn, d2 = together(normed_ffn, d2)
    d3 = hop(d2)
    forward = feed(normed_ffn, rest_full, ff_width)
    d_branch_all = jnp.concatenate([d_branch, d1, d2, d3], axis=0)
    grads_down = row_grads(d_branch_all, forward, 2, 1)
    forward, grads_down = together(forward, grads_down)
    grads_down = lax.psum_scatter(grads_down, "dp", scatter_dimension=0, tiled=True)
    y1, y2, y3, y0 = down(forward, down_full, (1, 2, 3, 0), width, size)
    y1, forward = together(y1, forward)
    y_sum = hop(y1)
    d_all = feed_back(d_branch_all, down_full, forward)
    (b1,) = back_feed(d_all, rest_full, (1,), width, size)
    b1, y_sum = together(b1, y_sum)
    b_sum = hop(b1)
    grads_feed = row_grads(normed_ffn, d_all, 0, 2)
    d_all, grads_feed = together(d_all, grads_feed)
    b2, b3, b0 = back_feed(d_all, rest_full, (2, 3, 0), width, size)
    b_sum, grads_feed, grads_down = together(add(b2, b_sum), grads_feed, grads_down)
    grads_feed = lax.psum_scatter(grads_feed, "dp", scatter_dimension=0, tiled=True)
    b_sum = hop(b_sum)
    b_sum, y_sum = together(hop(add(b3, b_sum)), y_sum)
    y_sum = hop(add(y2, y_sum))

    d_hidden, d_attended, p0, p1, p2, p3 = branch(
        (b0, b_sum), hidden, cotangent, own_live, norm_ffn_all, rest_full, q_width
    )
    p1, p2, p3, y_sum = together(p1, p2, p3, y_sum)
    grads_out = row_grads(d_attended, ctx_rows[None], 0, 1)
    s1, s2, s3, grads_out = together(
        shift_by(p3, 1), shift_by(p2, 2), shift_by(p1, -1), grads_out
    )
    d_q, d_k, d_v, sum_q, sum_k = attend_back(
        place_ref, qkv, [p0, s1, s2, s3], log_total, pre, cos, sin, gain_q, gain_k
    )
    d_q, grads_out, grads_feed = together(d_q, grads_out, grads_feed)
    grads_out = lax.psum_scatter(grads_out, "dp", scatter_dimension=0, tiled=True)
    parts = (d_q, d_k, d_v)
    e1, e2, e3, e0 = back_project(parts, attn_full, width, size)
    e_sum, d_q = together(e1, d_q)
    parts = (d_q, d_k, d_v)
    e_sum = hop(e_sum)
    grads_attn, norm_part = attend_grads(normed_attn, parts, attn_full)
    own_ffn = jnp.sum(
        w_gate.astype(f32) * grads_feed[:, :ff_width].astype(f32)
        + w_up.astype(f32) * grads_feed[:, ff_width:].astype(f32),
        axis=1,
    ) / norm_ffn.astype(f32)
    small = jnp.concatenate(
        [
            norm_part[:, 0] / norm_attn_all[0],
            own_ffn,
            sum_q[0, :HEAD_SIZE] + sum_q[0, HEAD_SIZE:],
            sum_k[0, :HEAD_SIZE] + sum_k[0, HEAD_SIZE:],
        ]
    )
    small = small + shift_by(small, 1) + shift_by(small, 2) + shift_by(small, 3)
    grad_norm_ffn = small[width : width + shard_rows]
    spread = lambda v: jnp.pad(
        v.reshape(data_ways, gain_rows), ((0, 0), (0, shard_rows - gain_rows))
    ).reshape(-1, 1)
    grads_attn = jnp.concatenate(
        [
            grads_attn,
            small[:width, None].astype(bf16),
            spread(small[width + shard_rows : width + shard_rows + HEAD_SIZE]).astype(bf16),
            spread(small[width + shard_rows + HEAD_SIZE :]).astype(bf16),
            jnp.zeros((width, 125), bf16),
        ],
        axis=1,
    )
    e_sum = hop(add(e2, e_sum))
    e_sum = hop(add(e3, e_sum))
    grads_attn, grads_out, e_sum, y_sum = together(
        grads_attn, grads_out, e_sum, add(y3, y_sum)
    )
    grads_attn = lax.psum_scatter(grads_attn, "dp", scatter_dimension=0, tiled=True)
    d_normed_attn = e0.astype(f32) + e_sum.astype(f32)

    y_sum = hop(y_sum)
    ffn_out = y0.astype(f32) + y_sum.astype(f32)
    block_out = ((hidden + ffn_out) * own_live).astype(bf16)
    own_tokens = tokens.astype(f32)
    d_tokens = d_hidden + norm_back(d_normed_attn, own_tokens, rms_scale(own_tokens), norm_attn_all)

    grads_feed = grads_feed.astype(f32)
    grad_gate, grad_up = grads_feed[:, :ff_width], grads_feed[:, ff_width:]
    grad_down = grads_down.astype(f32).T
    grad_qkv = grads_attn[:, :qkv_width].astype(f32)
    grad_query = grad_qkv[:, :q_width]
    grad_key = grad_qkv[:, q_width : q_width + kv_width]
    grad_value = grad_qkv[:, q_width + kv_width :]
    grad_norm_attn = grads_attn[:, qkv_width].astype(f32)
    grad_gain_query = grads_attn[:gain_rows, qkv_width + 1].astype(f32)
    grad_gain_key = grads_attn[:gain_rows, qkv_width + 2].astype(f32)
    g0, g1, g2, g3 = [grads_out[:, k * q_width : (k + 1) * q_width] for k in range(WAYS)]
    grad_output = (
        g0.astype(f32)
        + shift_by(g1, -1).astype(f32)
        + shift_by(g2, 2).astype(f32)
        + shift_by(g3, 1).astype(f32)
    ).T
    return (
        block_out,
        d_tokens.astype(bf16),
        grad_norm_attn,
        grad_query,
        grad_key,
        grad_value,
        grad_gain_query,
        grad_gain_key,
        grad_output,
        grad_norm_ffn,
        grad_gate,
        grad_up,
        grad_down,
    )


def solution(mesh):
    return jax.shard_map(
        local,
        mesh=mesh,
        in_specs=(
            P(("dp", "tensor"), None),
            P("dp"),
            P("dp", "tensor"),
            P("dp", "tensor"),
            P("dp", "tensor"),
            P("dp"),
            P("dp"),
            P("tensor", "dp"),
            P("dp"),
            P("dp", "tensor"),
            P("dp", "tensor"),
            P("tensor", "dp"),
            P(("dp", "tensor"), None),
            P(),
            P(),
        ),
        out_specs=(
            P(("dp", "tensor"), None),
            P(("dp", "tensor"), None),
            P("dp"),
            P("dp", "tensor"),
            P("dp", "tensor"),
            P("dp", "tensor"),
            P("dp"),
            P("dp"),
            P("tensor", "dp"),
            P("dp"),
            P("dp", "tensor"),
            P("dp", "tensor"),
            P("tensor", "dp"),
        ),
        check_vma=False,
    )
```

```python
import functools

import jax
import jax.numpy as jnp
from jax import lax
from jax.experimental import pallas as pl
from jax.experimental.pallas import tpu as pltpu
from jax.sharding import PartitionSpec as P

QUERY_HEADS = 16
KEY_VALUE_HEADS = 8
HEAD_SIZE = 128

norm_eps = 1e-06
rope_base = 1000000.0
score_scale = HEAD_SIZE ** (-0.5)
f32 = jnp.float32
bf16 = jnp.bfloat16
WAYS = 4
ROOM = 58 << 20


def nn(left, right):
    return lax.dot_general(left, right, (((1,), (0,)), ((), ())), preferred_element_type=f32)


def nt(left, right):
    return lax.dot_general(left, right, (((1,), (1,)), ((), ())), preferred_element_type=f32)


def tn(left, right):
    return lax.dot_general(left, right, (((0,), (0,)), ((), ())), preferred_element_type=f32)


def rms_scale(value_vectors):
    return lax.rsqrt(jnp.mean(value_vectors * value_vectors, axis=-1, keepdims=True) + norm_eps)


def norm_back(d_unit, pre_values, pre_scale, gain_values):
    mixed_terms = gain_values * d_unit
    return pre_scale * mixed_terms - pre_values * pre_scale**3 * jnp.mean(
        mixed_terms * pre_values, axis=-1, keepdims=True
    )


def rope_tables(position):
    half_dim = HEAD_SIZE // 2
    inverse_freq = rope_base ** (-2.0 * jnp.arange(half_dim, dtype=f32) / HEAD_SIZE)
    angles = position.astype(f32)[:, None] * inverse_freq[None, :]
    cosine, sine = jnp.cos(angles), jnp.sin(angles)
    return jnp.concatenate([cosine, cosine], axis=1), jnp.concatenate([-sine, sine], axis=1)


def sequence_length(lengths, deal_order, group_id):
    slots = jnp.arange(deal_order.shape[0], dtype=jnp.int32)
    seq_taken = jnp.sum(jnp.where(slots == group_id, deal_order, 0))
    return jnp.sum(jnp.where(slots == seq_taken, lengths, 0))


def shift_by(value, step):
    return lax.ppermute(value, "tensor", [(i, (i + step) % WAYS) for i in range(WAYS)])


def hop(value):
    return shift_by(value, 1)


def together(*values):
    return lax.optimization_barrier(values)


def add(block, arrived):
    return (block.astype(f32) + arrived.astype(f32)).astype(bf16)


def whole(shape, index=None):
    rank = len(shape)
    place = index if index is not None else (0,) * rank
    return pl.BlockSpec(shape, lambda *_: place, pipeline_mode=pl.Buffered(1))


def call(kernel, grid, in_specs, outs, out_specs, scratch=(), flops=0, size=0, exps=0):
    return pl.pallas_call(
        kernel,
        grid=grid,
        in_specs=in_specs,
        out_shape=[jax.ShapeDtypeStruct(s, d) for s, d in outs],
        out_specs=out_specs,
        scratch_shapes=list(scratch),
        compiler_params=pltpu.CompilerParams(vmem_limit_bytes=ROOM),
        cost_estimate=pl.CostEstimate(flops=flops, bytes_accessed=size, transcendentals=exps),
    )


def pick_slot(step, slots, x_s):
    for j, ref in enumerate(slots):

        @pl.when(step == j)
        def _():
            x_s[...] = ref[...]


def project_kernel(own, below, far, above, w, gain, gain_q, gain_k, cos, sin, normed, qkv, pre, x_s):
    pick_slot(pl.program_id(0), (own, below, far, above), x_s)
    x = x_s[...].astype(f32)
    n = (x * rms_scale(x) * gain[...]).astype(bf16)
    normed[...] = n
    projected = nn(n, w[...])
    heads = pre.shape[1] // HEAD_SIZE
    queries = heads * 2 // 3
    pre[...] = projected[:, : heads * HEAD_SIZE]
    c, s = cos[...], sin[...]
    for h in range(heads):
        cols = slice(h * HEAD_SIZE, (h + 1) * HEAD_SIZE)
        head = projected[:, cols]
        unit = head * rms_scale(head) * (gain_q[...] if h < queries else gain_k[...])
        qkv[:, cols] = (unit * c + pltpu.roll(unit, HEAD_SIZE // 2, 1) * s).astype(bf16)
    qkv[:, heads * HEAD_SIZE :] = projected[:, heads * HEAD_SIZE :].astype(bf16)


def project(x_slots, w, gain, gain_q, gain_k, cos, sin):
    rows, width = x_slots[0].shape
    cols = 1024
    pre_cols = 768
    tile = lambda c: pl.BlockSpec((rows, c), lambda j: (j, 0))
    return call(
        project_kernel,
        (WAYS,),
        [whole(x.shape) for x in x_slots]
        + [whole((width, cols)), whole(gain.shape), whole(gain_q.shape), whole(gain_k.shape)]
        + [tile(HEAD_SIZE), tile(HEAD_SIZE)],
        [((WAYS * rows, width), bf16), ((WAYS * rows, cols), bf16), ((WAYS * rows, pre_cols), f32)],
        [tile(width), tile(cols), tile(pre_cols)],
        [pltpu.VMEM((rows, width), bf16)],
        flops=2 * WAYS * rows * width * cols,
        size=20 << 20,
    )(*x_slots, w, gain, gain_q, gain_k, cos, sin)


def shard_starts(place, size):
    return [pl.multiple_of(lax.rem(place[0] + WAYS - s, WAYS) * size, size) for s in range(WAYS)]


def causal_fill(scores):
    row = lax.broadcasted_iota(jnp.int32, scores.shape, 0)
    col = lax.broadcasted_iota(jnp.int32, scores.shape, 1)
    return jnp.where(col <= row, scores, -1e30)


def attend_kernel(place, q, k, v, ctx, lse):
    size = q.shape[0] // WAYS
    starts = shard_starts(place, size)
    for s in range(WAYS):
        rows = pl.ds(starts[s], size)
        for g in range(q.shape[1] // HEAD_SIZE):
            cols = slice(g * HEAD_SIZE, (g + 1) * HEAD_SIZE)
            query = q[rows, cols]
            blocks = []
            for t in range(s + 1):
                scores = nt(query, k[pl.ds(starts[t], size), :])
                blocks.append(causal_fill(scores) if t == s else scores)
            top = functools.reduce(
                jnp.maximum, [jnp.max(b, axis=-1, keepdims=True) for b in blocks]
            )
            raised = [jnp.exp((b - top) * score_scale) for b in blocks]
            summed = functools.reduce(
                jnp.add, [jnp.sum(b, axis=-1, keepdims=True) for b in raised]
            )
            inverse = 1.0 / summed
            out = functools.reduce(
                jnp.add,
                [
                    nn((b * inverse).astype(bf16), v[pl.ds(starts[t], size), :])
                    for t, b in enumerate(raised)
                ],
            )
            ctx[rows, cols] = out.astype(bf16)
            lse[rows, g : g + 1] = top * score_scale + jnp.log(summed)


def attend(place, qkv):
    rows = qkv.shape[0]
    pairs = 2
    return call(
        attend_kernel,
        (pairs,),
        [
            pl.BlockSpec(memory_space=pltpu.SMEM),
            pl.BlockSpec((rows, 2 * HEAD_SIZE), lambda p: (0, p)),
            pl.BlockSpec((rows, HEAD_SIZE), lambda p: (0, 4 + p)),
            pl.BlockSpec((rows, HEAD_SIZE), lambda p: (0, 6 + p)),
        ],
        [((rows, 4 * HEAD_SIZE), bf16), ((rows, 2 * HEAD_SIZE), f32)],
        [
            pl.BlockSpec((rows, 2 * HEAD_SIZE), lambda p: (0, p)),
            pl.BlockSpec((rows, HEAD_SIZE), lambda p: (0, p)),
        ],
        flops=8 * rows * rows * HEAD_SIZE,
        size=2 << 20,
        exps=2 * rows * rows,
    )(place, qkv, qkv, qkv)


def mix_kernel(own, below, far, above, c0, c1, c2, c3, wa, wb, gain, normed, hidden, ctx_rows, x_s, c_s):
    i = pl.program_id(0)
    size = own.shape[0]
    inner = c0.shape[1]
    pick_slot(i, (own, below, far, above), x_s)
    for k, ref in enumerate((c0, c1, c2, c3)):
        start = pl.multiple_of(lax.rem(i + WAYS - k, WAYS) * size, size)
        c_s[:, k * inner : (k + 1) * inner] = ref[pl.ds(start, size), :]
    wide = wa.shape[1]
    h = x_s[...].astype(f32) + nt(c_s[:, :wide], wa[...]) + nt(c_s[:, wide:], wb[...])
    normed[...] = (h * rms_scale(h) * gain[...]).astype(bf16)

    @pl.when(i == 0)
    def _():
        hidden[...] = h
        ctx_rows[...] = c_s[...]


def mix(x_slots, contexts, weights, gain):
    size, width = x_slots[0].shape
    rows, inner = contexts[0].shape
    cols = WAYS * inner
    return call(
        mix_kernel,
        (WAYS,),
        [whole(x.shape) for x in x_slots]
        + [whole(c.shape) for c in contexts]
        + [whole((width, cols // 2), (0, 3)), whole((width, cols // 2), (0, 4)), whole(gain.shape)],
        [((rows, width), bf16), ((size, width), f32), ((size, cols), bf16)],
        [pl.BlockSpec((size, width), lambda i: (i, 0)), whole((size, width)), whole((size, cols))],
        [pltpu.VMEM((size, width), bf16), pltpu.VMEM((size, cols), bf16)],
        flops=2 * rows * width * cols,
        size=24 << 20,
    )(*x_slots, *contexts, weights, weights, gain)


def feed_kernel(n, w_gate, w_up, out):
    size = 256
    for i in range(n.shape[0] // size):
        rows = slice(i * size, (i + 1) * size)
        gate = nn(n[rows], w_gate[...])
        up = nn(n[rows], w_up[...])
        sig = 1.0 / (1.0 + jnp.exp(-gate))
        silu = gate * sig
        out[0, rows] = (up * sig * (1.0 + gate * (1.0 - sig))).astype(bf16)
        out[1, rows] = silu.astype(bf16)
        out[2, rows] = (silu * up).astype(bf16)


def feed(normed, weights, ff_width):
    rows, width = normed.shape
    tile = 256
    tiles = ff_width // tile
    col = lambda c: pl.BlockSpec((width, tile), lambda j: (0, c * tiles + j))
    return call(
        feed_kernel,
        (tiles,),
        [whole((rows, width)), col(0), col(1)],
        [((3, rows, ff_width), bf16)],
        [pl.BlockSpec((3, rows, tile), lambda j: (0, 0, j))],
        flops=4 * rows * width * ff_width,
        size=26 << 20,
        exps=rows * ff_width,
    )(normed, weights, weights)[0]


def feed_back_kernel(d, w_down, slopes, out):
    size = 256
    for i in range(d.shape[0] // size):
        rows = slice(i * size, (i + 1) * size)
        d_act = nn(d[rows], w_down[...])
        out[0, rows] = (d_act * slopes[0, rows].astype(f32)).astype(bf16)
        out[1, rows] = (d_act * slopes[1, rows].astype(f32)).astype(bf16)


def feed_back(d_branch, w_down, forward):
    rows, width = d_branch.shape
    ff_width = forward.shape[2]
    tile = 256
    return call(
        feed_back_kernel,
        (ff_width // tile,),
        [
            whole((rows, width)),
            pl.BlockSpec((width, tile), lambda j: (0, j)),
            pl.BlockSpec((2, rows, tile), lambda j: (0, 0, j)),
        ],
        [((2, rows, ff_width), bf16)],
        [pl.BlockSpec((2, rows, tile), lambda j: (0, 0, j))],
        flops=2 * rows * width * ff_width,
        size=22 << 20,
    )(d_branch, w_down, forward)[0]


def back_kernel(slots, size, lone, a, b, wa, wb, *outs):
    for slot, out in zip(slots, outs):
        rows = slice(0, size) if lone else slice(slot * size, (slot + 1) * size)
        out[...] = (nt(a[0, rows], wa[...]) + nt(b[0, rows], wb[...])).astype(bf16)


def slot_shapes(slots, size, width, tile):
    return [((size, width), bf16) for _ in slots], [
        pl.BlockSpec((size, tile), lambda n: (0, n)) for _ in slots
    ]


def back_feed(d_all, weights, slots, width, size):
    ff_width = d_all.shape[2]
    tile = 512
    lone = len(slots) == 1
    rows = size if lone else WAYS * size
    row_at = slots[0] if lone else 0
    outs, out_specs = slot_shapes(slots, size, width, tile)
    return call(
        functools.partial(back_kernel, slots, size, lone),
        (width // tile,),
        [
            whole((1, rows, ff_width), (0, row_at, 0)),
            whole((1, rows, ff_width), (1, row_at, 0)),
            pl.BlockSpec((tile, ff_width), lambda n: (n, 0)),
            pl.BlockSpec((tile, ff_width), lambda n: (n, 1)),
        ],
        outs,
        out_specs,
        flops=4 * len(slots) * size * width * ff_width,
        size=20 << 20,
    )(d_all, d_all, weights, weights)


def down_kernel(slots, size, a, wa, *outs):
    for slot, out in zip(slots, outs):
        out[...] = nt(a[0, slot * size : (slot + 1) * size], wa[...]).astype(bf16)


def down(d_all, weights, slots, width, size):
    ff_width = d_all.shape[2]
    tile = 512
    rows = WAYS * size
    outs, out_specs = slot_shapes(slots, size, width, tile)
    return call(
        functools.partial(down_kernel, slots, size),
        (width // tile,),
        [whole((1, rows, ff_width), (2, 0, 0)), pl.BlockSpec((tile, ff_width), lambda n: (n, 0))],
        outs,
        out_specs,
        flops=2 * rows * width * ff_width,
        size=14 << 20,
    )(d_all, weights)


def grads_kernel(n, a, out):
    width = a.shape[2]
    n_tile = n[...]
    for c in range(a.shape[0]):
        out[:, c * width : (c + 1) * width] = tn(n_tile, a[c]).astype(bf16)


def row_grads(left, right, first, count):
    rows, width = left.shape
    cols = right.shape[2]
    tile = 512
    return call(
        grads_kernel,
        (width // tile,),
        [
            pl.BlockSpec((rows, tile), lambda j: (0, j)),
            whole((count, rows, cols), (first // count, 0, 0)),
        ],
        [((width, count * cols), bf16)],
        [pl.BlockSpec((tile, count * cols), lambda j: (j, 0))],
        flops=2 * rows * width * cols * count,
        size=(4 + 9 * count) << 20,
    )(left, right)[0]


def branch_kernel(own, arrived, hidden, cotangent, live, gain, w, d_hidden, d_attended, c0, c1, c2, c3):
    k = pl.program_id(0)

    @pl.when(k == 0)
    def _():
        d_normed = own[...].astype(f32) + arrived[...].astype(f32)
        h = hidden[...]
        total = cotangent[...].astype(f32) * live[...] + norm_back(
            d_normed, h, rms_scale(h), gain[...]
        )
        d_hidden[...] = total
        d_attended[...] = total.astype(bf16)

    value = nn(d_attended[...], w[...]).astype(bf16)
    for kk, ref in enumerate((c0, c1, c2, c3)):

        @pl.when(k == kk)
        def _():
            ref[...] = value


def branch(parts, hidden, cotangent, live, gain, rest_full, inner):
    size, width = hidden.shape
    return call(
        branch_kernel,
        (WAYS,),
        [whole((size, width))] * 4
        + [whole(live.shape), whole(gain.shape), pl.BlockSpec((width, inner), lambda k: (0, 6 + k))],
        [((size, width), f32), ((size, width), bf16)] + [((size, inner), bf16)] * WAYS,
        [whole((size, width))] * 2 + [whole((size, inner))] * WAYS,
        flops=2 * size * width * WAYS * inner,
        size=16 << 20,
    )(*parts, hidden, cotangent, live, gain, rest_full)


def head_back(d_head, pre_head, gain, c, s):
    d_unit = d_head * c - pltpu.roll(d_head, HEAD_SIZE // 2, 1) * s
    scale = rms_scale(pre_head)
    return norm_back(d_unit, pre_head, scale, gain), jnp.sum(
        d_unit * pre_head * scale, axis=0, keepdims=True
    )


def attend_back_kernel(place, q, k, v, d0, d1, d2, d3, lse, pre_q, pre_k, cos, sin, gain_q, gain_k, dq_out, dk_out, dv_out, sum_q, sum_k, d_s, dk, dv):
    size = q.shape[0] // WAYS
    starts = shard_starts(place, size)
    for slot, ref in enumerate((d0, d1, d2, d3)):
        d_s[slot * size : (slot + 1) * size] = ref[...]
    dk[...] = jnp.zeros_like(dk)
    dv[...] = jnp.zeros_like(dv)
    total_q = jnp.zeros((1, HEAD_SIZE), f32)
    for s in range(WAYS):
        rows = pl.ds(starts[s], size)
        for g in range(q.shape[1] // HEAD_SIZE):
            cols = slice(g * HEAD_SIZE, (g + 1) * HEAD_SIZE)
            query, d_out, log_total = q[rows, cols], d_s[rows, cols], lse[rows, g : g + 1]
            probs, d_probs = [], []
            for t in range(s + 1):
                seen = pl.ds(starts[t], size)
                scores = nt(query, k[seen, :]) * score_scale
                scores = causal_fill(scores) if t == s else scores
                probs.append(jnp.exp(scores - log_total))
                d_probs.append(nt(d_out, v[seen, :]))
            row_dot = functools.reduce(
                jnp.add, [jnp.sum(p * d, axis=-1, keepdims=True) for p, d in zip(probs, d_probs)]
            )
            d_query = jnp.zeros((size, HEAD_SIZE), f32)
            for t in range(s + 1):
                seen = pl.ds(starts[t], size)
                d_scores = (probs[t] * (d_probs[t] - row_dot)).astype(bf16)
                dv[seen, :] += tn(probs[t].astype(bf16), d_out)
                dk[seen, :] += tn(d_scores, query)
                d_query += nn(d_scores, k[seen, :])
            d_pre, part = head_back(
                d_query * score_scale, pre_q[rows, cols], gain_q[...], cos[rows, :], sin[rows, :]
            )
            dq_out[rows, cols] = d_pre.astype(bf16)
            total_q += part
    d_pre, part = head_back(dk[...] * score_scale, pre_k[...], gain_k[...], cos[...], sin[...])
    dk_out[...] = d_pre.astype(bf16)
    dv_out[...] = dv[...].astype(bf16)
    sum_q[...] = jnp.broadcast_to(total_q, sum_q.shape)
    sum_k[...] = jnp.broadcast_to(part, sum_k.shape)


def attend_back(place, qkv, d_slots, lse, pre, cos, sin, gain_q, gain_k):
    rows = qkv.shape[0]
    size = rows // WAYS
    one, two = HEAD_SIZE, 2 * HEAD_SIZE
    cols = lambda r, c, at=0: pl.BlockSpec((r, c), lambda p: (0, at + p))
    return call(
        attend_back_kernel,
        (2,),
        [pl.BlockSpec(memory_space=pltpu.SMEM), cols(rows, two), cols(rows, one, 4), cols(rows, one, 6)]
        + [cols(size, two)] * WAYS
        + [cols(rows, one), cols(rows, two), cols(rows, one, 4)]
        + [whole((rows, one)), whole((rows, one)), whole((1, one)), whole((1, one))],
        [
            ((rows, 2 * two), bf16),
            ((rows, two), bf16),
            ((rows, two), bf16),
            ((8, two), f32),
            ((8, two), f32),
        ],
        [cols(rows, two), cols(rows, one), cols(rows, one), cols(8, one), cols(8, one)],
        [pltpu.VMEM((rows, two), bf16), pltpu.VMEM((rows, one), f32), pltpu.VMEM((rows, one), f32)],
        flops=40 * rows * rows * HEAD_SIZE,
        size=12 << 20,
        exps=4 * rows * rows,
    )(place, qkv, qkv, qkv, *d_slots, lse, pre, pre, cos, sin, gain_q, gain_k)


def back_project_kernel(lone, slots, size, q, k, v, w, *outs):
    for slot, out in zip(slots, outs):
        rows = slice(0, size) if lone else slice(slot * size, (slot + 1) * size)
        total, at = 0.0, 0
        for ref in (q, k, v):
            total += nt(ref[rows], w[:, at : at + ref.shape[1]])
            at += ref.shape[1]
        out[...] = total.astype(bf16)


def back_project(parts, w, slots, width, size):
    tile = 512
    lone = len(slots) == 1
    rows = size if lone else WAYS * size
    outs, out_specs = slot_shapes(slots, size, width, tile)
    return call(
        functools.partial(back_project_kernel, lone, slots, size),
        (width // tile,),
        [whole((rows, p.shape[1]), (slots[0] if lone else 0, 0)) for p in parts]
        + [pl.BlockSpec((tile, 1024), lambda n: (n, 0))],
        outs,
        out_specs,
        flops=2 * len(slots) * size * width * 1024,
        size=10 << 20,
    )(*parts, w)


def attend_grads_kernel(n, q, k, v, w, out, gain_part):
    n_tile = n[...]
    at = 0
    total = jnp.zeros(gain_part.shape, f32)
    for ref in (q, k, v):
        cols = slice(at, at + ref.shape[1])
        product = tn(n_tile, ref[...])
        out[:, cols] = product.astype(bf16)
        total += jnp.sum(product * w[:, cols].astype(f32), axis=1, keepdims=True)
        at += ref.shape[1]
    out[:, at:] = jnp.zeros((out.shape[0], out.shape[1] - at), bf16)
    gain_part[...] = total


def attend_grads(normed, parts, w):
    rows, width = normed.shape
    tile = 512
    cols = sum(p.shape[1] for p in parts)
    return call(
        attend_grads_kernel,
        (width // tile,),
        [pl.BlockSpec((rows, tile), lambda j: (0, j))]
        + [whole(p.shape) for p in parts]
        + [pl.BlockSpec((tile, cols), lambda j: (j, 0))],
        [((width, cols + 128), bf16), ((width, 128), f32)],
        [pl.BlockSpec((tile, cols + 128), lambda j: (j, 0)), pl.BlockSpec((tile, 128), lambda j: (j, 0))],
        flops=2 * rows * width * 1024,
        size=16 << 20,
    )(normed, *parts, w)


def local(
    tokens,
    norm_attn,
    w_query,
    key_matrix,
    value_matrix,
    gain_query,
    gain_key,
    w_output,
    norm_ffn,
    w_gate,
    w_up,
    w_down,
    cotangent,
    lengths,
    deal_order,
):
    place = lax.axis_index("tensor")
    data_ways = lax.axis_size("dp")
    size, width = tokens.shape
    shard_rows = norm_attn.shape[0]
    gain_rows = gain_query.shape[0]
    q_width = w_query.shape[1]
    kv_width = key_matrix.shape[1]
    qkv_width = q_width + 2 * kv_width
    ff_width = w_gate.shape[1]
    place_ref = place.reshape(1).astype(jnp.int32)

    w_out = w_output.T
    x1, w1, w3 = together(hop(tokens), hop(w_out), shift_by(w_out, -1))
    offsets = jnp.arange(size, dtype=jnp.int32)
    position = jnp.concatenate([((place - j) % WAYS) * size + offsets for j in range(WAYS)])
    cos, sin = rope_tables(position)
    seq_len = sequence_length(lengths, deal_order, lax.axis_index("dp"))
    own_live = (position[:size] < seq_len).astype(f32)[:, None]
    d_branch = (cotangent.astype(f32) * own_live).astype(bf16)
    x2, w2, cos, sin, d_branch = together(hop(x1), hop(w1), cos, sin, d_branch)
    x3, d_branch = together(hop(x2), d_branch)
    x_slots = [tokens, x1, x2, x3]
    d1 = hop(d_branch)

    column = lambda v: jnp.pad(v, (0, shard_rows - v.shape[0]))[:, None]
    attn_part = jnp.concatenate(
        [w_query, key_matrix, value_matrix]
        + [column(v) for v in (norm_attn, norm_ffn, gain_query, gain_key)]
        + [jnp.zeros((shard_rows, 124), bf16)],
        axis=1,
    )
    attn_full = lax.all_gather(attn_part, "dp", axis=0, tiled=True)
    gain_block = attn_full[:, qkv_width : qkv_width + 4].astype(f32)
    norm_attn_all = gain_block[:, 0].reshape(1, width)
    norm_ffn_all = gain_block[:, 1].reshape(1, width)
    by_shard = gain_block.reshape(data_ways, shard_rows, 4)[:, :gain_rows]
    gain_q = by_shard[:, :, 2].reshape(1, HEAD_SIZE)
    gain_k = by_shard[:, :, 3].reshape(1, HEAD_SIZE)

    rest_full = lax.all_gather(
        jnp.concatenate([w_gate, w_up, w_out, w1, w2, w3], axis=1), "dp", axis=0, tiled=True
    )
    w_down_part, x2 = together(w_down.T, x2)
    x_slots = [tokens, x1, x2, x3]
    down_full = lax.all_gather(w_down_part, "dp", axis=0, tiled=True)

    normed_attn, qkv, pre = project(x_slots, attn_full, norm_attn_all, gain_q, gain_k, cos, sin)
    context, log_total = attend(place_ref, qkv)
    context, d1 = together(context, d1)
    c1 = hop(context)
    c2 = hop(c1)
    c3, d1 = together(hop(c2), d1)
    d2 = hop(d1)
    normed_ffn, hidden, ctx_rows = mix(x_slots, [context, c1, c2, c3], rest_full, norm_ffn_all)

    normed_ffn, d2 = together(normed_ffn, d2)
    d3 = hop(d2)
    forward = feed(normed_ffn, rest_full, ff_width)
    d_branch_all = jnp.concatenate([d_branch, d1, d2, d3], axis=0)
    grads_down = row_grads(d_branch_all, forward, 2, 1)
    forward, grads_down = together(forward, grads_down)
    grads_down = lax.psum_scatter(grads_down, "dp", scatter_dimension=0, tiled=True)
    y1, y2, y3, y0 = down(forward, down_full, (1, 2, 3, 0), width, size)
    y1, forward = together(y1, forward)
    y_sum = hop(y1)
    d_all = feed_back(d_branch_all, down_full, forward)
    (b1,) = back_feed(d_all, rest_full, (1,), width, size)
    b1, y_sum = together(b1, y_sum)
    b_sum = hop(b1)
    b2, b3, b0 = back_feed(d_all, rest_full, (2, 3, 0), width, size)
    b_sum, d_all = together(add(b2, b_sum), d_all)
    b_sum = hop(b_sum)
    grads_feed = row_grads(normed_ffn, d_all, 0, 2)
    b_sum, grads_feed = together(b_sum, grads_feed)
    grads_feed, grads_down = together(grads_feed, grads_down)
    grads_feed = lax.psum_scatter(grads_feed, "dp", scatter_dimension=0, tiled=True)
    b_sum, y_sum = together(hop(add(b3, b_sum)), y_sum)
    y_sum = hop(add(y2, y_sum))

    d_hidden, d_attended, p0, p1, p2, p3 = branch(
        (b0, b_sum), hidden, cotangent, own_live, norm_ffn_all, rest_full, q_width
    )
    p1, p2, p3, y_sum = together(p1, p2, p3, y_sum)
    grads_out = row_grads(d_attended, ctx_rows[None], 0, 1)
    s1, s2, s3, grads_out = together(
        shift_by(p3, 1), shift_by(p2, 2), shift_by(p1, -1), grads_out
    )
    d_q, d_k, d_v, sum_q, sum_k = attend_back(
        place_ref, qkv, [p0, s1, s2, s3], log_total, pre, cos, sin, gain_q, gain_k
    )
    (e1,) = back_project((d_q, d_k, d_v), attn_full, (1,), width, size)
    e1, d_q, grads_out, grads_feed = together(e1, d_q, grads_out, grads_feed)
    grads_out = lax.psum_scatter(grads_out, "dp", scatter_dimension=0, tiled=True)
    e_sum = hop(e1)
    y_sum = hop(add(y3, y_sum))
    parts = (d_q, d_k, d_v)
    e2, e3, e0 = back_project(parts, attn_full, (2, 3, 0), width, size)
    grads_attn, norm_part = attend_grads(normed_attn, parts, attn_full)
    e_sum, grads_attn, norm_part, y_sum = together(
        add(e2, e_sum), grads_attn, norm_part, y_sum
    )
    e_sum = hop(e_sum)
    own_ffn = jnp.sum(
        w_gate.astype(f32) * grads_feed[:, :ff_width].astype(f32)
        + w_up.astype(f32) * grads_feed[:, ff_width:].astype(f32),
        axis=1,
    ) / norm_ffn.astype(f32)
    small = jnp.concatenate(
        [
            norm_part[:, 0] / norm_attn_all[0],
            own_ffn,
            sum_q[0, :HEAD_SIZE] + sum_q[0, HEAD_SIZE:],
            sum_k[0, :HEAD_SIZE] + sum_k[0, HEAD_SIZE:],
        ]
    )
    small = small + shift_by(small, 1) + shift_by(small, 2) + shift_by(small, 3)
    grad_norm_ffn = small[width : width + shard_rows]
    gain_row = jnp.concatenate(
        [
            small[width + shard_rows :].reshape(2, data_ways, 1, gain_rows)[0],
            small[width + shard_rows :].reshape(2, data_ways, 1, gain_rows)[1],
            jnp.zeros((data_ways, 1, 127 - 2 * gain_rows), f32),
        ],
        axis=2,
    )
    gain_columns = jnp.concatenate(
        [
            small[:width].reshape(data_ways, shard_rows, 1),
            jnp.pad(gain_row, ((0, 0), (0, shard_rows - 1), (0, 0))),
        ],
        axis=2,
    ).reshape(width, 128).astype(bf16)
    grads_attn = lax.dynamic_update_slice(grads_attn, gain_columns, (0, qkv_width))
    grads_attn, grads_out, e_sum = together(grads_attn, grads_out, add(e3, e_sum))
    e_sum = hop(e_sum)
    grads_attn = lax.psum_scatter(grads_attn, "dp", scatter_dimension=0, tiled=True)
    d_normed_attn = e0.astype(f32) + e_sum.astype(f32)

    ffn_out = y0.astype(f32) + y_sum.astype(f32)
    block_out = ((hidden + ffn_out) * own_live).astype(bf16)
    own_tokens = tokens.astype(f32)
    d_tokens = d_hidden + norm_back(d_normed_attn, own_tokens, rms_scale(own_tokens), norm_attn_all)

    grads_feed = grads_feed.astype(f32)
    grad_gate, grad_up = grads_feed[:, :ff_width], grads_feed[:, ff_width:]
    grad_down = grads_down.astype(f32).T
    grad_qkv = grads_attn[:, :qkv_width].astype(f32)
    grad_query = grad_qkv[:, :q_width]
    grad_key = grad_qkv[:, q_width : q_width + kv_width]
    grad_value = grad_qkv[:, q_width + kv_width :]
    grad_norm_attn = grads_attn[:, qkv_width].astype(f32)
    gain_at = qkv_width + 1
    grad_gain_query = grads_attn[0, gain_at : gain_at + gain_rows].astype(f32)
    grad_gain_key = grads_attn[0, gain_at + gain_rows : gain_at + 2 * gain_rows].astype(f32)
    g0, g1, g2, g3 = [grads_out[:, k * q_width : (k + 1) * q_width] for k in range(WAYS)]
    g0, d_tokens = together(g0, d_tokens.astype(bf16))
    grad_output = (
        g0.astype(f32)
        + shift_by(g1, -1).astype(f32)
        + shift_by(g2, 2).astype(f32)
        + shift_by(g3, 1).astype(f32)
    ).T
    return (
        block_out,
        d_tokens,
        grad_norm_attn,
        grad_query,
        grad_key,
        grad_value,
        grad_gain_query,
        grad_gain_key,
        grad_output,
        grad_norm_ffn,
        grad_gate,
        grad_up,
        grad_down,
    )


def solution(mesh):
    return jax.shard_map(
        local,
        mesh=mesh,
        in_specs=(
            P(("dp", "tensor"), None),
            P("dp"),
            P("dp", "tensor"),
            P("dp", "tensor"),
            P("dp", "tensor"),
            P("dp"),
            P("dp"),
            P("tensor", "dp"),
            P("dp"),
            P("dp", "tensor"),
            P("dp", "tensor"),
            P("tensor", "dp"),
            P(("dp", "tensor"), None),
            P(),
            P(),
        ),
        out_specs=(
            P(("dp", "tensor"), None),
            P(("dp", "tensor"), None),
            P("dp"),
            P("dp", "tensor"),
            P("dp", "tensor"),
            P("dp", "tensor"),
            P("dp"),
            P("dp"),
            P("tensor", "dp"),
            P("dp"),
            P("dp", "tensor"),
            P("dp", "tensor"),
            P("tensor", "dp"),
        ),
        check_vma=False,
    )
```

```python
import functools

import jax
import jax.numpy as jnp
from jax import lax
from jax.experimental import pallas as pl
from jax.experimental.pallas import tpu as pltpu
from jax.sharding import PartitionSpec as P

QUERY_HEADS = 16
KEY_VALUE_HEADS = 8
HEAD_SIZE = 128

norm_eps = 1e-06
rope_base = 1000000.0
score_scale = HEAD_SIZE ** (-0.5)
f32 = jnp.float32
bf16 = jnp.bfloat16
WAYS = 4
ROOM = 58 << 20


def nn(left, right):
    return lax.dot_general(left, right, (((1,), (0,)), ((), ())), preferred_element_type=f32)


def nt(left, right):
    return lax.dot_general(left, right, (((1,), (1,)), ((), ())), preferred_element_type=f32)


def tn(left, right):
    return lax.dot_general(left, right, (((0,), (0,)), ((), ())), preferred_element_type=f32)


def rms_scale(value_vectors):
    return lax.rsqrt(jnp.mean(value_vectors * value_vectors, axis=-1, keepdims=True) + norm_eps)


def norm_back(d_unit, pre_values, pre_scale, gain_values):
    mixed_terms = gain_values * d_unit
    return pre_scale * mixed_terms - pre_values * pre_scale**3 * jnp.mean(
        mixed_terms * pre_values, axis=-1, keepdims=True
    )


def rope_tables(position):
    half_dim = HEAD_SIZE // 2
    inverse_freq = rope_base ** (-2.0 * jnp.arange(half_dim, dtype=f32) / HEAD_SIZE)
    angles = position.astype(f32)[:, None] * inverse_freq[None, :]
    cosine, sine = jnp.cos(angles), jnp.sin(angles)
    return jnp.concatenate([cosine, cosine], axis=1), jnp.concatenate([-sine, sine], axis=1)


def sequence_length(lengths, deal_order, group_id):
    slots = jnp.arange(deal_order.shape[0], dtype=jnp.int32)
    seq_taken = jnp.sum(jnp.where(slots == group_id, deal_order, 0))
    return jnp.sum(jnp.where(slots == seq_taken, lengths, 0))


def shift_by(value, step):
    return lax.ppermute(value, "tensor", [(i, (i + step) % WAYS) for i in range(WAYS)])


def hop(value):
    return shift_by(value, 1)


def together(*values):
    return lax.optimization_barrier(values)


def add(block, arrived):
    return (block.astype(f32) + arrived.astype(f32)).astype(bf16)


def whole(shape, index=None):
    rank = len(shape)
    place = index if index is not None else (0,) * rank
    return pl.BlockSpec(shape, lambda *_: place, pipeline_mode=pl.Buffered(1))


def call(kernel, grid, in_specs, outs, out_specs, scratch=(), flops=0, size=0, exps=0):
    return pl.pallas_call(
        kernel,
        grid=grid,
        in_specs=in_specs,
        out_shape=[jax.ShapeDtypeStruct(s, d) for s, d in outs],
        out_specs=out_specs,
        scratch_shapes=list(scratch),
        compiler_params=pltpu.CompilerParams(vmem_limit_bytes=ROOM),
        cost_estimate=pl.CostEstimate(flops=flops, bytes_accessed=size, transcendentals=exps),
    )


def pick_slot(step, slots, x_s):
    for j, ref in enumerate(slots):

        @pl.when(step == j)
        def _():
            x_s[...] = ref[...]


def project_kernel(own, below, far, above, w, gain, gain_q, gain_k, cos, sin, normed, qkv, pre, x_s):
    pick_slot(pl.program_id(0), (own, below, far, above), x_s)
    x = x_s[...].astype(f32)
    n = (x * rms_scale(x) * gain[...]).astype(bf16)
    normed[...] = n
    projected = nn(n, w[...])
    heads = pre.shape[1] // HEAD_SIZE
    queries = heads * 2 // 3
    pre[...] = projected[:, : heads * HEAD_SIZE]
    c, s = cos[...], sin[...]
    for h in range(heads):
        cols = slice(h * HEAD_SIZE, (h + 1) * HEAD_SIZE)
        head = projected[:, cols]
        unit = head * rms_scale(head) * (gain_q[...] if h < queries else gain_k[...])
        qkv[:, cols] = (unit * c + pltpu.roll(unit, HEAD_SIZE // 2, 1) * s).astype(bf16)
    qkv[:, heads * HEAD_SIZE :] = projected[:, heads * HEAD_SIZE :].astype(bf16)


def project(x_slots, w, gain, gain_q, gain_k, cos, sin):
    rows, width = x_slots[0].shape
    cols = 1024
    pre_cols = 768
    tile = lambda c: pl.BlockSpec((rows, c), lambda j: (j, 0))
    return call(
        project_kernel,
        (WAYS,),
        [whole(x.shape) for x in x_slots]
        + [whole((width, cols)), whole(gain.shape), whole(gain_q.shape), whole(gain_k.shape)]
        + [tile(HEAD_SIZE), tile(HEAD_SIZE)],
        [((WAYS * rows, width), bf16), ((WAYS * rows, cols), bf16), ((WAYS * rows, pre_cols), f32)],
        [tile(width), tile(cols), tile(pre_cols)],
        [pltpu.VMEM((rows, width), bf16)],
        flops=2 * WAYS * rows * width * cols,
        size=20 << 20,
    )(*x_slots, w, gain, gain_q, gain_k, cos, sin)


def shard_starts(place, size):
    return [pl.multiple_of(lax.rem(place[0] + WAYS - s, WAYS) * size, size) for s in range(WAYS)]


def causal_fill(scores):
    row = lax.broadcasted_iota(jnp.int32, scores.shape, 0)
    col = lax.broadcasted_iota(jnp.int32, scores.shape, 1)
    return jnp.where(col <= row, scores, -1e30)


def attend_kernel(place, q, k, v, ctx, lse):
    size = q.shape[0] // WAYS
    starts = shard_starts(place, size)
    for s in range(WAYS):
        rows = pl.ds(starts[s], size)
        for g in range(q.shape[1] // HEAD_SIZE):
            cols = slice(g * HEAD_SIZE, (g + 1) * HEAD_SIZE)
            query = q[rows, cols]
            blocks = []
            for t in range(s + 1):
                scores = nt(query, k[pl.ds(starts[t], size), :])
                blocks.append(causal_fill(scores) if t == s else scores)
            top = functools.reduce(
                jnp.maximum, [jnp.max(b, axis=-1, keepdims=True) for b in blocks]
            )
            raised = [jnp.exp((b - top) * score_scale) for b in blocks]
            summed = functools.reduce(
                jnp.add, [jnp.sum(b, axis=-1, keepdims=True) for b in raised]
            )
            inverse = 1.0 / summed
            out = functools.reduce(
                jnp.add,
                [
                    nn((b * inverse).astype(bf16), v[pl.ds(starts[t], size), :])
                    for t, b in enumerate(raised)
                ],
            )
            ctx[rows, cols] = out.astype(bf16)
            lse[rows, g : g + 1] = top * score_scale + jnp.log(summed)


def attend(place, qkv):
    rows = qkv.shape[0]
    pairs = 2
    return call(
        attend_kernel,
        (pairs,),
        [
            pl.BlockSpec(memory_space=pltpu.SMEM),
            pl.BlockSpec((rows, 2 * HEAD_SIZE), lambda p: (0, p)),
            pl.BlockSpec((rows, HEAD_SIZE), lambda p: (0, 4 + p)),
            pl.BlockSpec((rows, HEAD_SIZE), lambda p: (0, 6 + p)),
        ],
        [((rows, 4 * HEAD_SIZE), bf16), ((rows, 2 * HEAD_SIZE), f32)],
        [
            pl.BlockSpec((rows, 2 * HEAD_SIZE), lambda p: (0, p)),
            pl.BlockSpec((rows, HEAD_SIZE), lambda p: (0, p)),
        ],
        flops=8 * rows * rows * HEAD_SIZE,
        size=2 << 20,
        exps=2 * rows * rows,
    )(place, qkv, qkv, qkv)


def mix_kernel(own, below, far, above, c0, c1, c2, c3, wa, wb, gain, normed, hidden, ctx_rows, acc, c_s):
    n = pl.program_id(0)
    size, tile = own.shape
    inner = c0.shape[1]
    wide = wa.shape[1]
    tiles = acc.shape[0]

    @pl.when(n == 0)
    def _():
        for k, ref in enumerate((c0, c1, c2, c3)):
            for i in range(WAYS):
                source = (i - k) % WAYS
                c_s[i * size : (i + 1) * size, k * inner : (k + 1) * inner] = ref[
                    source * size : (source + 1) * size
                ]
        ctx_rows[...] = c_s[:size]

    for i, x in enumerate((own, below, far, above)):
        rows = slice(i * size, (i + 1) * size)
        acc[n, rows] = (
            x[...].astype(f32) + nt(c_s[rows, :wide], wa[...]) + nt(c_s[rows, wide:], wb[...])
        )

    @pl.when(n == tiles - 1)
    def _():
        for i in range(WAYS):
            rows = slice(i * size, (i + 1) * size)
            squares = sum(
                jnp.sum(acc[m, rows] * acc[m, rows], axis=-1, keepdims=True) for m in range(tiles)
            )
            scale = lax.rsqrt(squares / (tiles * tile) + norm_eps)
            for m in range(tiles):
                cols = slice(m * tile, (m + 1) * tile)
                normed[rows, cols] = (acc[m, rows] * scale * gain[:, cols]).astype(bf16)
                if i == 0:
                    hidden[:, cols] = acc[m, rows]


def mix(x_slots, contexts, weights, gain):
    size, width = x_slots[0].shape
    rows, inner = contexts[0].shape
    cols = WAYS * inner
    tile = 512
    return call(
        mix_kernel,
        (width // tile,),
        [pl.BlockSpec((size, tile), lambda n: (0, n)) for _ in x_slots]
        + [whole(c.shape) for c in contexts]
        + [pl.BlockSpec((tile, cols // 2), lambda n: (n, 3))]
        + [pl.BlockSpec((tile, cols // 2), lambda n: (n, 4)), whole(gain.shape)],
        [((rows, width), bf16), ((size, width), f32), ((size, cols), bf16)],
        [whole((rows, width)), whole((size, width)), whole((size, cols))],
        [pltpu.VMEM((width // tile, rows, tile), f32), pltpu.VMEM((rows, cols), bf16)],
        flops=2 * rows * width * cols,
        size=24 << 20,
    )(*x_slots, *contexts, weights, weights, gain)


def feed_kernel(n, w_gate, w_up, out):
    size = 256
    for i in range(n.shape[0] // size):
        rows = slice(i * size, (i + 1) * size)
        gate = nn(n[rows], w_gate[...])
        up = nn(n[rows], w_up[...])
        sig = 1.0 / (1.0 + jnp.exp(-gate))
        silu = gate * sig
        out[0, rows] = (up * sig * (1.0 + gate * (1.0 - sig))).astype(bf16)
        out[1, rows] = silu.astype(bf16)
        out[2, rows] = (silu * up).astype(bf16)


def feed(normed, weights, ff_width):
    rows, width = normed.shape
    tile = 256
    tiles = ff_width // tile
    col = lambda c: pl.BlockSpec((width, tile), lambda j: (0, c * tiles + j))
    return call(
        feed_kernel,
        (tiles,),
        [whole((rows, width)), col(0), col(1)],
        [((3, rows, ff_width), bf16)],
        [pl.BlockSpec((3, rows, tile), lambda j: (0, 0, j))],
        flops=4 * rows * width * ff_width,
        size=26 << 20,
        exps=rows * ff_width,
    )(normed, weights, weights)[0]


def feed_back_kernel(d, w_down, slopes, out):
    size = 256
    for i in range(d.shape[0] // size):
        rows = slice(i * size, (i + 1) * size)
        d_act = nn(d[rows], w_down[...])
        out[0, rows] = (d_act * slopes[0, rows].astype(f32)).astype(bf16)
        out[1, rows] = (d_act * slopes[1, rows].astype(f32)).astype(bf16)


def feed_back(d_branch, w_down, forward):
    rows, width = d_branch.shape
    ff_width = forward.shape[2]
    tile = 512
    return call(
        feed_back_kernel,
        (ff_width // tile,),
        [
            whole((rows, width)),
            pl.BlockSpec((width, tile), lambda j: (0, j)),
            pl.BlockSpec((2, rows, tile), lambda j: (0, 0, j)),
        ],
        [((2, rows, ff_width), bf16)],
        [pl.BlockSpec((2, rows, tile), lambda j: (0, 0, j))],
        flops=2 * rows * width * ff_width,
        size=22 << 20,
    )(d_branch, w_down, forward)[0]


def back_kernel(slots, size, lone, a, b, wa, wb, *outs):
    for slot, out in zip(slots, outs):
        rows = slice(0, size) if lone else slice(slot * size, (slot + 1) * size)
        out[...] = (nt(a[0, rows], wa[...]) + nt(b[0, rows], wb[...])).astype(bf16)


def slot_shapes(slots, size, width, tile):
    return [((size, width), bf16) for _ in slots], [
        pl.BlockSpec((size, tile), lambda n: (0, n)) for _ in slots
    ]


def back_feed(d_all, weights, slots, width, size):
    ff_width = d_all.shape[2]
    tile = 512
    lone = len(slots) == 1
    rows = size if lone else WAYS * size
    row_at = slots[0] if lone else 0
    outs, out_specs = slot_shapes(slots, size, width, tile)
    return call(
        functools.partial(back_kernel, slots, size, lone),
        (width // tile,),
        [
            whole((1, rows, ff_width), (0, row_at, 0)),
            whole((1, rows, ff_width), (1, row_at, 0)),
            pl.BlockSpec((tile, ff_width), lambda n: (n, 0)),
            pl.BlockSpec((tile, ff_width), lambda n: (n, 1)),
        ],
        outs,
        out_specs,
        flops=4 * len(slots) * size * width * ff_width,
        size=20 << 20,
    )(d_all, d_all, weights, weights)


def down_kernel(slots, size, a, wa, *outs):
    for slot, out in zip(slots, outs):
        out[...] = nt(a[0, slot * size : (slot + 1) * size], wa[...]).astype(bf16)


def down(d_all, weights, slots, width, size):
    ff_width = d_all.shape[2]
    tile = 512
    rows = WAYS * size
    outs, out_specs = slot_shapes(slots, size, width, tile)
    return call(
        functools.partial(down_kernel, slots, size),
        (width // tile,),
        [whole((1, rows, ff_width), (2, 0, 0)), pl.BlockSpec((tile, ff_width), lambda n: (n, 0))],
        outs,
        out_specs,
        flops=2 * rows * width * ff_width,
        size=14 << 20,
    )(d_all, weights)


def grads_kernel(n, a, out):
    width = a.shape[2]
    n_tile = n[...]
    for c in range(a.shape[0]):
        out[:, c * width : (c + 1) * width] = tn(n_tile, a[c]).astype(bf16)


def row_grads(left, right, first, count):
    rows, width = left.shape
    cols = right.shape[2]
    tile = 512
    return call(
        grads_kernel,
        (width // tile,),
        [
            pl.BlockSpec((rows, tile), lambda j: (0, j)),
            whole((count, rows, cols), (first // count, 0, 0)),
        ],
        [((width, count * cols), bf16)],
        [pl.BlockSpec((tile, count * cols), lambda j: (j, 0))],
        flops=2 * rows * width * cols * count,
        size=(4 + 9 * count) << 20,
    )(left, right)[0]


def branch_kernel(own, arrived, hidden, cotangent, live, gain, w, d_hidden, d_attended, c0, c1, c2, c3):
    k = pl.program_id(0)

    @pl.when(k == 0)
    def _():
        d_normed = own[...].astype(f32) + arrived[...].astype(f32)
        h = hidden[...]
        total = cotangent[...].astype(f32) * live[...] + norm_back(
            d_normed, h, rms_scale(h), gain[...]
        )
        d_hidden[...] = total
        d_attended[...] = total.astype(bf16)

    value = nn(d_attended[...], w[...]).astype(bf16)
    for kk, ref in enumerate((c0, c1, c2, c3)):

        @pl.when(k == kk)
        def _():
            ref[...] = value


def branch(parts, hidden, cotangent, live, gain, rest_full, inner):
    size, width = hidden.shape
    return call(
        branch_kernel,
        (WAYS,),
        [whole((size, width))] * 4
        + [whole(live.shape), whole(gain.shape), pl.BlockSpec((width, inner), lambda k: (0, 6 + k))],
        [((size, width), f32), ((size, width), bf16)] + [((size, inner), bf16)] * WAYS,
        [whole((size, width))] * 2 + [whole((size, inner))] * WAYS,
        flops=2 * size * width * WAYS * inner,
        size=16 << 20,
    )(*parts, hidden, cotangent, live, gain, rest_full)


def head_back(d_head, pre_head, gain, c, s):
    d_unit = d_head * c - pltpu.roll(d_head, HEAD_SIZE // 2, 1) * s
    scale = rms_scale(pre_head)
    return norm_back(d_unit, pre_head, scale, gain), jnp.sum(
        d_unit * pre_head * scale, axis=0, keepdims=True
    )


def attend_back_kernel(place, q, k, v, d0, d1, d2, d3, lse, pre_q, pre_k, cos, sin, gain_q, gain_k, dq_out, dk_out, dv_out, sum_q, sum_k, d_s, dk, dv):
    size = q.shape[0] // WAYS
    starts = shard_starts(place, size)
    for slot, ref in enumerate((d0, d1, d2, d3)):
        d_s[slot * size : (slot + 1) * size] = ref[...]
    dk[...] = jnp.zeros_like(dk)
    dv[...] = jnp.zeros_like(dv)
    total_q = jnp.zeros((1, HEAD_SIZE), f32)
    for s in range(WAYS):
        rows = pl.ds(starts[s], size)
        for g in range(q.shape[1] // HEAD_SIZE):
            cols = slice(g * HEAD_SIZE, (g + 1) * HEAD_SIZE)
            query, d_out, log_total = q[rows, cols], d_s[rows, cols], lse[rows, g : g + 1]
            probs, d_probs = [], []
            for t in range(s + 1):
                seen = pl.ds(starts[t], size)
                scores = nt(query, k[seen, :]) * score_scale
                scores = causal_fill(scores) if t == s else scores
                probs.append(jnp.exp(scores - log_total))
                d_probs.append(nt(d_out, v[seen, :]))
            row_dot = functools.reduce(
                jnp.add, [jnp.sum(p * d, axis=-1, keepdims=True) for p, d in zip(probs, d_probs)]
            )
            d_query = jnp.zeros((size, HEAD_SIZE), f32)
            for t in range(s + 1):
                seen = pl.ds(starts[t], size)
                d_scores = (probs[t] * (d_probs[t] - row_dot)).astype(bf16)
                dv[seen, :] += tn(probs[t].astype(bf16), d_out)
                dk[seen, :] += tn(d_scores, query)
                d_query += nn(d_scores, k[seen, :])
            d_pre, part = head_back(
                d_query * score_scale, pre_q[rows, cols], gain_q[...], cos[rows, :], sin[rows, :]
            )
            dq_out[rows, cols] = d_pre.astype(bf16)
            total_q += part
    d_pre, part = head_back(dk[...] * score_scale, pre_k[...], gain_k[...], cos[...], sin[...])
    dk_out[...] = d_pre.astype(bf16)
    dv_out[...] = dv[...].astype(bf16)
    sum_q[...] = jnp.broadcast_to(total_q, sum_q.shape)
    sum_k[...] = jnp.broadcast_to(part, sum_k.shape)


def attend_back(place, qkv, d_slots, lse, pre, cos, sin, gain_q, gain_k):
    rows = qkv.shape[0]
    size = rows // WAYS
    one, two = HEAD_SIZE, 2 * HEAD_SIZE
    cols = lambda r, c, at=0: pl.BlockSpec((r, c), lambda p: (0, at + p))
    return call(
        attend_back_kernel,
        (2,),
        [pl.BlockSpec(memory_space=pltpu.SMEM), cols(rows, two), cols(rows, one, 4), cols(rows, one, 6)]
        + [cols(size, two)] * WAYS
        + [cols(rows, one), cols(rows, two), cols(rows, one, 4)]
        + [whole((rows, one)), whole((rows, one)), whole((1, one)), whole((1, one))],
        [
            ((rows, 2 * two), bf16),
            ((rows, two), bf16),
            ((rows, two), bf16),
            ((8, two), f32),
            ((8, two), f32),
        ],
        [cols(rows, two), cols(rows, one), cols(rows, one), cols(8, one), cols(8, one)],
        [pltpu.VMEM((rows, two), bf16), pltpu.VMEM((rows, one), f32), pltpu.VMEM((rows, one), f32)],
        flops=40 * rows * rows * HEAD_SIZE,
        size=12 << 20,
        exps=4 * rows * rows,
    )(place, qkv, qkv, qkv, *d_slots, lse, pre, pre, cos, sin, gain_q, gain_k)


def back_project_kernel(lone, slots, size, q, k, v, w, *outs):
    for slot, out in zip(slots, outs):
        rows = slice(0, size) if lone else slice(slot * size, (slot + 1) * size)
        total, at = 0.0, 0
        for ref in (q, k, v):
            total += nt(ref[rows], w[:, at : at + ref.shape[1]])
            at += ref.shape[1]
        out[...] = total.astype(bf16)


def back_project(parts, w, slots, width, size):
    tile = 512
    lone = len(slots) == 1
    rows = size if lone else WAYS * size
    outs, out_specs = slot_shapes(slots, size, width, tile)
    return call(
        functools.partial(back_project_kernel, lone, slots, size),
        (width // tile,),
        [whole((rows, p.shape[1]), (slots[0] if lone else 0, 0)) for p in parts]
        + [pl.BlockSpec((tile, 1024), lambda n: (n, 0))],
        outs,
        out_specs,
        flops=2 * len(slots) * size * width * 1024,
        size=10 << 20,
    )(*parts, w)


def attend_grads_kernel(n, q, k, v, w, out, gain_part):
    n_tile = n[...]
    at = 0
    total = jnp.zeros(gain_part.shape, f32)
    for ref in (q, k, v):
        cols = slice(at, at + ref.shape[1])
        product = tn(n_tile, ref[...])
        out[:, cols] = product.astype(bf16)
        total += jnp.sum(product * w[:, cols].astype(f32), axis=1, keepdims=True)
        at += ref.shape[1]
    out[:, at:] = jnp.zeros((out.shape[0], out.shape[1] - at), bf16)
    gain_part[...] = total


def attend_grads(normed, parts, w):
    rows, width = normed.shape
    tile = 512
    cols = sum(p.shape[1] for p in parts)
    return call(
        attend_grads_kernel,
        (width // tile,),
        [pl.BlockSpec((rows, tile), lambda j: (0, j))]
        + [whole(p.shape) for p in parts]
        + [pl.BlockSpec((tile, cols), lambda j: (j, 0))],
        [((width, cols + 128), bf16), ((width, 128), f32)],
        [pl.BlockSpec((tile, cols + 128), lambda j: (j, 0)), pl.BlockSpec((tile, 128), lambda j: (j, 0))],
        flops=2 * rows * width * 1024,
        size=16 << 20,
    )(normed, *parts, w)


def local(
    tokens,
    norm_attn,
    w_query,
    key_matrix,
    value_matrix,
    gain_query,
    gain_key,
    w_output,
    norm_ffn,
    w_gate,
    w_up,
    w_down,
    cotangent,
    lengths,
    deal_order,
):
    place = lax.axis_index("tensor")
    data_ways = lax.axis_size("dp")
    size, width = tokens.shape
    shard_rows = norm_attn.shape[0]
    gain_rows = gain_query.shape[0]
    q_width = w_query.shape[1]
    kv_width = key_matrix.shape[1]
    qkv_width = q_width + 2 * kv_width
    ff_width = w_gate.shape[1]
    place_ref = place.reshape(1).astype(jnp.int32)

    w_out = w_output.T
    x1, w1, w3 = together(hop(tokens), hop(w_out), shift_by(w_out, -1))
    offsets = jnp.arange(size, dtype=jnp.int32)
    position = jnp.concatenate([((place - j) % WAYS) * size + offsets for j in range(WAYS)])
    cos, sin = rope_tables(position)
    seq_len = sequence_length(lengths, deal_order, lax.axis_index("dp"))
    own_live = (position[:size] < seq_len).astype(f32)[:, None]
    d_branch = (cotangent.astype(f32) * own_live).astype(bf16)
    x2, w2, cos, sin, d_branch = together(hop(x1), hop(w1), cos, sin, d_branch)
    x3, d_branch = together(hop(x2), d_branch)
    x_slots = [tokens, x1, x2, x3]
    d1 = hop(d_branch)

    column = lambda v: jnp.pad(v, (0, shard_rows - v.shape[0]))[:, None]
    attn_part = jnp.concatenate(
        [w_query, key_matrix, value_matrix]
        + [column(v) for v in (norm_attn, norm_ffn, gain_query, gain_key)]
        + [jnp.zeros((shard_rows, 124), bf16)],
        axis=1,
    )
    attn_full = lax.all_gather(attn_part, "dp", axis=0, tiled=True)
    gain_block = attn_full[:, qkv_width : qkv_width + 4].astype(f32)
    norm_attn_all = gain_block[:, 0].reshape(1, width)
    norm_ffn_all = gain_block[:, 1].reshape(1, width)
    by_shard = gain_block.reshape(data_ways, shard_rows, 4)[:, :gain_rows]
    gain_q = by_shard[:, :, 2].reshape(1, HEAD_SIZE)
    gain_k = by_shard[:, :, 3].reshape(1, HEAD_SIZE)

    rest_full = lax.all_gather(
        jnp.concatenate([w_gate, w_up, w_out, w1, w2, w3], axis=1), "dp", axis=0, tiled=True
    )
    w_down_part, x2 = together(w_down.T, x2)
    x_slots = [tokens, x1, x2, x3]
    down_full = lax.all_gather(w_down_part, "dp", axis=0, tiled=True)

    normed_attn, qkv, pre = project(x_slots, attn_full, norm_attn_all, gain_q, gain_k, cos, sin)
    context, log_total = attend(place_ref, qkv)
    context, d1 = together(context, d1)
    c1 = hop(context)
    c2 = hop(c1)
    c3, d1 = together(hop(c2), d1)
    d2 = hop(d1)
    normed_ffn, hidden, ctx_rows = mix(x_slots, [context, c1, c2, c3], rest_full, norm_ffn_all)

    normed_ffn, d2 = together(normed_ffn, d2)
    d3 = hop(d2)
    forward = feed(normed_ffn, rest_full, ff_width)
    d_branch_all = jnp.concatenate([d_branch, d1, d2, d3], axis=0)
    grads_down = row_grads(d_branch_all, forward, 2, 1)
    forward, grads_down = together(forward, grads_down)
    grads_down = lax.psum_scatter(grads_down, "dp", scatter_dimension=0, tiled=True)
    y1, y2, y3, y0 = down(forward, down_full, (1, 2, 3, 0), width, size)
    y1, forward = together(y1, forward)
    y_sum = hop(y1)
    d_all = feed_back(d_branch_all, down_full, forward)
    (b1,) = back_feed(d_all, rest_full, (1,), width, size)
    b1, y_sum = together(b1, y_sum)
    b_sum = hop(b1)
    b2, b3, b0 = back_feed(d_all, rest_full, (2, 3, 0), width, size)
    b_sum, d_all = together(add(b2, b_sum), d_all)
    b_sum = hop(b_sum)
    grads_feed = row_grads(normed_ffn, d_all, 0, 2)
    b_sum, grads_feed = together(b_sum, grads_feed)
    grads_feed, grads_down = together(grads_feed, grads_down)
    grads_feed = lax.psum_scatter(grads_feed, "dp", scatter_dimension=0, tiled=True)
    b_sum, y_sum = together(hop(add(b3, b_sum)), y_sum)
    y_sum = hop(add(y2, y_sum))

    d_hidden, d_attended, p0, p1, p2, p3 = branch(
        (b0, b_sum), hidden, cotangent, own_live, norm_ffn_all, rest_full, q_width
    )
    grads_out = row_grads(d_attended, ctx_rows[None], 0, 1)
    s1, s2, s3, grads_out, y_sum = together(
        shift_by(p3, 1), shift_by(p2, 2), shift_by(p1, -1), grads_out, y_sum
    )
    d_q, d_k, d_v, sum_q, sum_k = attend_back(
        place_ref, qkv, [p0, s1, s2, s3], log_total, pre, cos, sin, gain_q, gain_k
    )
    (e1,) = back_project((d_q, d_k, d_v), attn_full, (1,), width, size)
    e1, d_q, grads_out, grads_feed = together(e1, d_q, grads_out, grads_feed)
    grads_out = lax.psum_scatter(grads_out, "dp", scatter_dimension=0, tiled=True)
    e_sum = hop(e1)
    y_sum = hop(add(y3, y_sum))
    parts = (d_q, d_k, d_v)
    e2, e3, e0 = back_project(parts, attn_full, (2, 3, 0), width, size)
    grads_attn, norm_part = attend_grads(normed_attn, parts, attn_full)
    e_sum, grads_attn, norm_part, y_sum = together(
        add(e2, e_sum), grads_attn, norm_part, y_sum
    )
    e_sum = hop(e_sum)
    own_ffn = jnp.sum(
        w_gate.astype(f32) * grads_feed[:, :ff_width].astype(f32)
        + w_up.astype(f32) * grads_feed[:, ff_width:].astype(f32),
        axis=1,
    ) / norm_ffn.astype(f32)
    small = jnp.concatenate(
        [
            norm_part[:, 0] / norm_attn_all[0],
            own_ffn,
            sum_q[0, :HEAD_SIZE] + sum_q[0, HEAD_SIZE:],
            sum_k[0, :HEAD_SIZE] + sum_k[0, HEAD_SIZE:],
        ]
    )
    small = small + shift_by(small, 1) + shift_by(small, 2) + shift_by(small, 3)
    grad_norm_ffn = small[width : width + shard_rows]
    gain_row = jnp.concatenate(
        [
            small[width + shard_rows :].reshape(2, data_ways, 1, gain_rows)[0],
            small[width + shard_rows :].reshape(2, data_ways, 1, gain_rows)[1],
            jnp.zeros((data_ways, 1, 127 - 2 * gain_rows), f32),
        ],
        axis=2,
    )
    gain_columns = jnp.concatenate(
        [
            small[:width].reshape(data_ways, shard_rows, 1),
            jnp.pad(gain_row, ((0, 0), (0, shard_rows - 1), (0, 0))),
        ],
        axis=2,
    ).reshape(width, 128).astype(bf16)
    grads_attn = lax.dynamic_update_slice(grads_attn, gain_columns, (0, qkv_width))
    grads_attn, grads_out, e_sum = together(grads_attn, grads_out, add(e3, e_sum))
    e_sum = hop(e_sum)
    grads_attn = lax.psum_scatter(grads_attn, "dp", scatter_dimension=0, tiled=True)
    d_normed_attn = e0.astype(f32) + e_sum.astype(f32)

    ffn_out = y0.astype(f32) + y_sum.astype(f32)
    block_out = ((hidden + ffn_out) * own_live).astype(bf16)
    own_tokens = tokens.astype(f32)
    d_tokens = d_hidden + norm_back(d_normed_attn, own_tokens, rms_scale(own_tokens), norm_attn_all)

    grads_feed = grads_feed.astype(f32)
    grad_gate, grad_up = grads_feed[:, :ff_width], grads_feed[:, ff_width:]
    grad_down = grads_down.astype(f32).T
    grad_qkv = grads_attn[:, :qkv_width].astype(f32)
    grad_query = grad_qkv[:, :q_width]
    grad_key = grad_qkv[:, q_width : q_width + kv_width]
    grad_value = grad_qkv[:, q_width + kv_width :]
    grad_norm_attn = grads_attn[:, qkv_width].astype(f32)
    gain_at = qkv_width + 1
    grad_gain_query = grads_attn[0, gain_at : gain_at + gain_rows].astype(f32)
    grad_gain_key = grads_attn[0, gain_at + gain_rows : gain_at + 2 * gain_rows].astype(f32)
    g0, g1, g2, g3 = [grads_out[:, k * q_width : (k + 1) * q_width] for k in range(WAYS)]
    g0, d_tokens = together(g0, d_tokens.astype(bf16))
    grad_output = (
        g0.astype(f32)
        + shift_by(g1, -1).astype(f32)
        + shift_by(g2, 2).astype(f32)
        + shift_by(g3, 1).astype(f32)
    ).T
    return (
        block_out,
        d_tokens,
        grad_norm_attn,
        grad_query,
        grad_key,
        grad_value,
        grad_gain_query,
        grad_gain_key,
        grad_output,
        grad_norm_ffn,
        grad_gate,
        grad_up,
        grad_down,
    )


def solution(mesh):
    return jax.shard_map(
        local,
        mesh=mesh,
        in_specs=(
            P(("dp", "tensor"), None),
            P("dp"),
            P("dp", "tensor"),
            P("dp", "tensor"),
            P("dp", "tensor"),
            P("dp"),
            P("dp"),
            P("tensor", "dp"),
            P("dp"),
            P("dp", "tensor"),
            P("dp", "tensor"),
            P("tensor", "dp"),
            P(("dp", "tensor"), None),
            P(),
            P(),
        ),
        out_specs=(
            P(("dp", "tensor"), None),
            P(("dp", "tensor"), None),
            P("dp"),
            P("dp", "tensor"),
            P("dp", "tensor"),
            P("dp", "tensor"),
            P("dp"),
            P("dp"),
            P("tensor", "dp"),
            P("dp"),
            P("dp", "tensor"),
            P("dp", "tensor"),
            P("tensor", "dp"),
        ),
        check_vma=False,
    )
```

```python
import functools

import jax
import jax.numpy as jnp
from jax import lax
from jax.experimental import pallas as pl
from jax.experimental.pallas import tpu as pltpu
from jax.sharding import PartitionSpec as P

QUERY_HEADS = 16
KEY_VALUE_HEADS = 8
HEAD_SIZE = 128

norm_eps = 1e-06
rope_base = 1000000.0
score_scale = HEAD_SIZE ** (-0.5)
f32 = jnp.float32
bf16 = jnp.bfloat16
WAYS = 4
ROOM = 58 << 20


def nn(left, right):
    return lax.dot_general(left, right, (((1,), (0,)), ((), ())), preferred_element_type=f32)


def nt(left, right):
    return lax.dot_general(left, right, (((1,), (1,)), ((), ())), preferred_element_type=f32)


def tn(left, right):
    return lax.dot_general(left, right, (((0,), (0,)), ((), ())), preferred_element_type=f32)


def rms_scale(value_vectors):
    return lax.rsqrt(jnp.mean(value_vectors * value_vectors, axis=-1, keepdims=True) + norm_eps)


def norm_back(d_unit, pre_values, pre_scale, gain_values):
    mixed_terms = gain_values * d_unit
    return pre_scale * mixed_terms - pre_values * pre_scale**3 * jnp.mean(
        mixed_terms * pre_values, axis=-1, keepdims=True
    )


def rope_tables(position):
    half_dim = HEAD_SIZE // 2
    inverse_freq = rope_base ** (-2.0 * jnp.arange(half_dim, dtype=f32) / HEAD_SIZE)
    angles = position.astype(f32)[:, None] * inverse_freq[None, :]
    cosine, sine = jnp.cos(angles), jnp.sin(angles)
    return jnp.concatenate([cosine, cosine], axis=1), jnp.concatenate([-sine, sine], axis=1)


def sequence_length(lengths, deal_order, group_id):
    slots = jnp.arange(deal_order.shape[0], dtype=jnp.int32)
    seq_taken = jnp.sum(jnp.where(slots == group_id, deal_order, 0))
    return jnp.sum(jnp.where(slots == seq_taken, lengths, 0))


def shift_by(value, step):
    return lax.ppermute(value, "tensor", [(i, (i + step) % WAYS) for i in range(WAYS)])


def hop(value):
    return shift_by(value, 1)


def together(*values):
    return lax.optimization_barrier(values)


def add(block, arrived):
    return (block.astype(f32) + arrived.astype(f32)).astype(bf16)


def whole(shape, index=None):
    rank = len(shape)
    place = index if index is not None else (0,) * rank
    return pl.BlockSpec(shape, lambda *_: place, pipeline_mode=pl.Buffered(1))


def call(kernel, grid, in_specs, outs, out_specs, scratch=(), flops=0, size=0, exps=0):
    return pl.pallas_call(
        kernel,
        grid=grid,
        in_specs=in_specs,
        out_shape=[jax.ShapeDtypeStruct(s, d) for s, d in outs],
        out_specs=out_specs,
        scratch_shapes=list(scratch),
        compiler_params=pltpu.CompilerParams(vmem_limit_bytes=ROOM),
        cost_estimate=pl.CostEstimate(flops=flops, bytes_accessed=size, transcendentals=exps),
    )


def pick_slot(step, slots, x_s):
    for j, ref in enumerate(slots):

        @pl.when(step == j)
        def _():
            x_s[...] = ref[...]


def project_kernel(own, below, far, above, w, gain, gain_q, gain_k, cos, sin, normed, qkv, pre, x_s):
    pick_slot(pl.program_id(0), (own, below, far, above), x_s)
    x = x_s[...].astype(f32)
    n = (x * rms_scale(x) * gain[...]).astype(bf16)
    normed[...] = n
    projected = nn(n, w[...])
    heads = pre.shape[1] // HEAD_SIZE
    queries = heads * 2 // 3
    pre[...] = projected[:, : heads * HEAD_SIZE]
    c, s = cos[...], sin[...]
    for h in range(heads):
        cols = slice(h * HEAD_SIZE, (h + 1) * HEAD_SIZE)
        head = projected[:, cols]
        unit = head * rms_scale(head) * (gain_q[...] if h < queries else gain_k[...])
        qkv[:, cols] = (unit * c + pltpu.roll(unit, HEAD_SIZE // 2, 1) * s).astype(bf16)
    qkv[:, heads * HEAD_SIZE :] = projected[:, heads * HEAD_SIZE :].astype(bf16)


def project(x_slots, w, gain, gain_q, gain_k, cos, sin):
    rows, width = x_slots[0].shape
    cols = 1024
    pre_cols = 768
    tile = lambda c: pl.BlockSpec((rows, c), lambda j: (j, 0))
    return call(
        project_kernel,
        (WAYS,),
        [whole(x.shape) for x in x_slots]
        + [whole((width, cols)), whole(gain.shape), whole(gain_q.shape), whole(gain_k.shape)]
        + [tile(HEAD_SIZE), tile(HEAD_SIZE)],
        [((WAYS * rows, width), bf16), ((WAYS * rows, cols), bf16), ((WAYS * rows, pre_cols), f32)],
        [tile(width), tile(cols), tile(pre_cols)],
        [pltpu.VMEM((rows, width), bf16)],
        flops=2 * WAYS * rows * width * cols,
        size=20 << 20,
    )(*x_slots, w, gain, gain_q, gain_k, cos, sin)


def shard_starts(place, size):
    return [pl.multiple_of(lax.rem(place[0] + WAYS - s, WAYS) * size, size) for s in range(WAYS)]


def causal_fill(scores):
    row = lax.broadcasted_iota(jnp.int32, scores.shape, 0)
    col = lax.broadcasted_iota(jnp.int32, scores.shape, 1)
    return jnp.where(col <= row, scores, -1e30)


def attend_kernel(place, q, k, v, ctx, lse):
    size = q.shape[0] // WAYS
    starts = shard_starts(place, size)
    for s in range(WAYS):
        rows = pl.ds(starts[s], size)
        for g in range(q.shape[1] // HEAD_SIZE):
            cols = slice(g * HEAD_SIZE, (g + 1) * HEAD_SIZE)
            query = q[rows, cols]
            blocks = []
            for t in range(s + 1):
                scores = nt(query, k[pl.ds(starts[t], size), :])
                blocks.append(causal_fill(scores) if t == s else scores)
            top = functools.reduce(
                jnp.maximum, [jnp.max(b, axis=-1, keepdims=True) for b in blocks]
            )
            raised = [jnp.exp((b - top) * score_scale) for b in blocks]
            summed = functools.reduce(
                jnp.add, [jnp.sum(b, axis=-1, keepdims=True) for b in raised]
            )
            inverse = 1.0 / summed
            out = functools.reduce(
                jnp.add,
                [
                    nn((b * inverse).astype(bf16), v[pl.ds(starts[t], size), :])
                    for t, b in enumerate(raised)
                ],
            )
            ctx[rows, cols] = out.astype(bf16)
            lse[rows, g : g + 1] = top * score_scale + jnp.log(summed)


def attend(place, qkv):
    rows = qkv.shape[0]
    pairs = 2
    return call(
        attend_kernel,
        (pairs,),
        [
            pl.BlockSpec(memory_space=pltpu.SMEM),
            pl.BlockSpec((rows, 2 * HEAD_SIZE), lambda p: (0, p)),
            pl.BlockSpec((rows, HEAD_SIZE), lambda p: (0, 4 + p)),
            pl.BlockSpec((rows, HEAD_SIZE), lambda p: (0, 6 + p)),
        ],
        [((rows, 4 * HEAD_SIZE), bf16), ((rows, 2 * HEAD_SIZE), f32)],
        [
            pl.BlockSpec((rows, 2 * HEAD_SIZE), lambda p: (0, p)),
            pl.BlockSpec((rows, HEAD_SIZE), lambda p: (0, p)),
        ],
        flops=8 * rows * rows * HEAD_SIZE,
        size=2 << 20,
        exps=2 * rows * rows,
    )(place, qkv, qkv, qkv)


def mix_kernel(own, below, far, above, c0, c1, c2, c3, wa, wb, gain, normed, hidden, ctx_rows, x_s, c_s):
    i = pl.program_id(0)
    size = own.shape[0]
    inner = c0.shape[1]
    pick_slot(i, (own, below, far, above), x_s)
    for k, ref in enumerate((c0, c1, c2, c3)):
        start = pl.multiple_of(lax.rem(i + WAYS - k, WAYS) * size, size)
        c_s[:, k * inner : (k + 1) * inner] = ref[pl.ds(start, size), :]
    wide = wa.shape[1]
    h = x_s[...].astype(f32) + nt(c_s[:, :wide], wa[...]) + nt(c_s[:, wide:], wb[...])
    normed[...] = (h * rms_scale(h) * gain[...]).astype(bf16)

    @pl.when(i == 0)
    def _():
        hidden[...] = h
        ctx_rows[...] = c_s[...]


def mix(x_slots, contexts, weights, gain):
    size, width = x_slots[0].shape
    rows, inner = contexts[0].shape
    cols = WAYS * inner
    return call(
        mix_kernel,
        (WAYS,),
        [whole(x.shape) for x in x_slots]
        + [whole(c.shape) for c in contexts]
        + [whole((width, cols // 2), (0, 3)), whole((width, cols // 2), (0, 4)), whole(gain.shape)],
        [((rows, width), bf16), ((size, width), f32), ((size, cols), bf16)],
        [pl.BlockSpec((size, width), lambda i: (i, 0)), whole((size, width)), whole((size, cols))],
        [pltpu.VMEM((size, width), bf16), pltpu.VMEM((size, cols), bf16)],
        flops=2 * rows * width * cols,
        size=24 << 20,
    )(*x_slots, *contexts, weights, weights, gain)


def feed_kernel(n, w_gate, w_up, out):
    size = 256
    for i in range(n.shape[0] // size):
        rows = slice(i * size, (i + 1) * size)
        gate = nn(n[rows], w_gate[...])
        up = nn(n[rows], w_up[...])
        sig = 1.0 / (1.0 + jnp.exp(-gate))
        silu = gate * sig
        out[0, rows] = (up * sig * (1.0 + gate * (1.0 - sig))).astype(bf16)
        out[1, rows] = silu.astype(bf16)
        out[2, rows] = (silu * up).astype(bf16)


def feed(normed, weights, ff_width):
    rows, width = normed.shape
    tile = 256
    tiles = ff_width // tile
    col = lambda c: pl.BlockSpec((width, tile), lambda j: (0, c * tiles + j))
    return call(
        feed_kernel,
        (tiles,),
        [whole((rows, width)), col(0), col(1)],
        [((3, rows, ff_width), bf16)],
        [pl.BlockSpec((3, rows, tile), lambda j: (0, 0, j))],
        flops=4 * rows * width * ff_width,
        size=26 << 20,
        exps=rows * ff_width,
    )(normed, weights, weights)[0]


def feed_back_kernel(d, w_down, slopes, out):
    size = 256
    for i in range(d.shape[0] // size):
        rows = slice(i * size, (i + 1) * size)
        d_act = nn(d[rows], w_down[...])
        out[0, rows] = (d_act * slopes[0, rows].astype(f32)).astype(bf16)
        out[1, rows] = (d_act * slopes[1, rows].astype(f32)).astype(bf16)


def feed_back(d_branch, w_down, forward):
    rows, width = d_branch.shape
    ff_width = forward.shape[2]
    tile = 256
    return call(
        feed_back_kernel,
        (ff_width // tile,),
        [
            whole((rows, width)),
            pl.BlockSpec((width, tile), lambda j: (0, j)),
            pl.BlockSpec((2, rows, tile), lambda j: (0, 0, j)),
        ],
        [((2, rows, ff_width), bf16)],
        [pl.BlockSpec((2, rows, tile), lambda j: (0, 0, j))],
        flops=2 * rows * width * ff_width,
        size=22 << 20,
    )(d_branch, w_down, forward)[0]


def back_kernel(slots, size, lone, a, b, wa, wb, *outs):
    for slot, out in zip(slots, outs):
        rows = slice(0, size) if lone else slice(slot * size, (slot + 1) * size)
        out[...] = (nt(a[0, rows], wa[...]) + nt(b[0, rows], wb[...])).astype(bf16)


def slot_shapes(slots, size, width, tile):
    return [((size, width), bf16) for _ in slots], [
        pl.BlockSpec((size, tile), lambda n: (0, n)) for _ in slots
    ]


def back_feed(d_all, weights, slots, width, size):
    ff_width = d_all.shape[2]
    tile = 512
    lone = len(slots) == 1
    rows = size if lone else WAYS * size
    row_at = slots[0] if lone else 0
    outs, out_specs = slot_shapes(slots, size, width, tile)
    return call(
        functools.partial(back_kernel, slots, size, lone),
        (width // tile,),
        [
            whole((1, rows, ff_width), (0, row_at, 0)),
            whole((1, rows, ff_width), (1, row_at, 0)),
            pl.BlockSpec((tile, ff_width), lambda n: (n, 0)),
            pl.BlockSpec((tile, ff_width), lambda n: (n, 1)),
        ],
        outs,
        out_specs,
        flops=4 * len(slots) * size * width * ff_width,
        size=20 << 20,
    )(d_all, d_all, weights, weights)


def down_kernel(slots, size, a, wa, *outs):
    for slot, out in zip(slots, outs):
        out[...] = nt(a[0, slot * size : (slot + 1) * size], wa[...]).astype(bf16)


def down(d_all, weights, slots, width, size):
    ff_width = d_all.shape[2]
    tile = 512
    rows = WAYS * size
    outs, out_specs = slot_shapes(slots, size, width, tile)
    return call(
        functools.partial(down_kernel, slots, size),
        (width // tile,),
        [whole((1, rows, ff_width), (2, 0, 0)), pl.BlockSpec((tile, ff_width), lambda n: (n, 0))],
        outs,
        out_specs,
        flops=2 * rows * width * ff_width,
        size=14 << 20,
    )(d_all, weights)


def grads_kernel(n, a, out):
    width = a.shape[2]
    n_tile = n[...]
    for c in range(a.shape[0]):
        out[:, c * width : (c + 1) * width] = tn(n_tile, a[c]).astype(bf16)


def row_grads(left, right, first, count):
    rows, width = left.shape
    cols = right.shape[2]
    tile = 512
    return call(
        grads_kernel,
        (width // tile,),
        [
            pl.BlockSpec((rows, tile), lambda j: (0, j)),
            whole((count, rows, cols), (first // count, 0, 0)),
        ],
        [((width, count * cols), bf16)],
        [pl.BlockSpec((tile, count * cols), lambda j: (j, 0))],
        flops=2 * rows * width * cols * count,
        size=(4 + 9 * count) << 20,
    )(left, right)[0]


def branch_kernel(own, arrived, hidden, cotangent, live, gain, w, d_hidden, d_attended, c0, c1, c2, c3):
    k = pl.program_id(0)

    @pl.when(k == 0)
    def _():
        d_normed = own[...].astype(f32) + arrived[...].astype(f32)
        h = hidden[...]
        total = cotangent[...].astype(f32) * live[...] + norm_back(
            d_normed, h, rms_scale(h), gain[...]
        )
        d_hidden[...] = total
        d_attended[...] = total.astype(bf16)

    value = nn(d_attended[...], w[...]).astype(bf16)
    for kk, ref in enumerate((c0, c1, c2, c3)):

        @pl.when(k == kk)
        def _():
            ref[...] = value


def branch(parts, hidden, cotangent, live, gain, rest_full, inner):
    size, width = hidden.shape
    return call(
        branch_kernel,
        (WAYS,),
        [whole((size, width))] * 4
        + [whole(live.shape), whole(gain.shape), pl.BlockSpec((width, inner), lambda k: (0, 6 + k))],
        [((size, width), f32), ((size, width), bf16)] + [((size, inner), bf16)] * WAYS,
        [whole((size, width))] * 2 + [whole((size, inner))] * WAYS,
        flops=2 * size * width * WAYS * inner,
        size=16 << 20,
    )(*parts, hidden, cotangent, live, gain, rest_full)


def head_back(d_head, pre_head, gain, c, s):
    d_unit = d_head * c - pltpu.roll(d_head, HEAD_SIZE // 2, 1) * s
    scale = rms_scale(pre_head)
    return norm_back(d_unit, pre_head, scale, gain), jnp.sum(
        d_unit * pre_head * scale, axis=0, keepdims=True
    )


def attend_back_kernel(place, q, k, v, d0, d1, d2, d3, lse, pre_q, pre_k, cos, sin, gain_q, gain_k, dq_out, dk_out, dv_out, sum_q, sum_k, d_s, dk, dv):
    size = q.shape[0] // WAYS
    starts = shard_starts(place, size)
    for slot, ref in enumerate((d0, d1, d2, d3)):
        d_s[slot * size : (slot + 1) * size] = ref[...]
    dk[...] = jnp.zeros_like(dk)
    dv[...] = jnp.zeros_like(dv)
    total_q = jnp.zeros((1, HEAD_SIZE), f32)
    for s in range(WAYS):
        rows = pl.ds(starts[s], size)
        for g in range(q.shape[1] // HEAD_SIZE):
            cols = slice(g * HEAD_SIZE, (g + 1) * HEAD_SIZE)
            query, d_out, log_total = q[rows, cols], d_s[rows, cols], lse[rows, g : g + 1]
            probs, d_probs = [], []
            for t in range(s + 1):
                seen = pl.ds(starts[t], size)
                scores = nt(query, k[seen, :]) * score_scale
                scores = causal_fill(scores) if t == s else scores
                probs.append(jnp.exp(scores - log_total))
                d_probs.append(nt(d_out, v[seen, :]))
            row_dot = functools.reduce(
                jnp.add, [jnp.sum(p * d, axis=-1, keepdims=True) for p, d in zip(probs, d_probs)]
            )
            d_query = jnp.zeros((size, HEAD_SIZE), f32)
            for t in range(s + 1):
                seen = pl.ds(starts[t], size)
                d_scores = (probs[t] * (d_probs[t] - row_dot)).astype(bf16)
                dv[seen, :] += tn(probs[t].astype(bf16), d_out)
                dk[seen, :] += tn(d_scores, query)
                d_query += nn(d_scores, k[seen, :])
            d_pre, part = head_back(
                d_query * score_scale, pre_q[rows, cols], gain_q[...], cos[rows, :], sin[rows, :]
            )
            dq_out[rows, cols] = d_pre.astype(bf16)
            total_q += part
    d_pre, part = head_back(dk[...] * score_scale, pre_k[...], gain_k[...], cos[...], sin[...])
    dk_out[...] = d_pre.astype(bf16)
    dv_out[...] = dv[...].astype(bf16)
    sum_q[...] = jnp.broadcast_to(total_q, sum_q.shape)
    sum_k[...] = jnp.broadcast_to(part, sum_k.shape)


def attend_back(place, qkv, d_slots, lse, pre, cos, sin, gain_q, gain_k):
    rows = qkv.shape[0]
    size = rows // WAYS
    one, two = HEAD_SIZE, 2 * HEAD_SIZE
    cols = lambda r, c, at=0: pl.BlockSpec((r, c), lambda p: (0, at + p))
    return call(
        attend_back_kernel,
        (2,),
        [pl.BlockSpec(memory_space=pltpu.SMEM), cols(rows, two), cols(rows, one, 4), cols(rows, one, 6)]
        + [cols(size, two)] * WAYS
        + [cols(rows, one), cols(rows, two), cols(rows, one, 4)]
        + [whole((rows, one)), whole((rows, one)), whole((1, one)), whole((1, one))],
        [
            ((rows, 2 * two), bf16),
            ((rows, two), bf16),
            ((rows, two), bf16),
            ((8, two), f32),
            ((8, two), f32),
        ],
        [cols(rows, two), cols(rows, one), cols(rows, one), cols(8, one), cols(8, one)],
        [pltpu.VMEM((rows, two), bf16), pltpu.VMEM((rows, one), f32), pltpu.VMEM((rows, one), f32)],
        flops=40 * rows * rows * HEAD_SIZE,
        size=12 << 20,
        exps=4 * rows * rows,
    )(place, qkv, qkv, qkv, *d_slots, lse, pre, pre, cos, sin, gain_q, gain_k)


def back_project_kernel(lone, slots, size, q, k, v, w, *outs):
    for slot, out in zip(slots, outs):
        rows = slice(0, size) if lone else slice(slot * size, (slot + 1) * size)
        total, at = 0.0, 0
        for ref in (q, k, v):
            total += nt(ref[rows], w[:, at : at + ref.shape[1]])
            at += ref.shape[1]
        out[...] = total.astype(bf16)


def back_project(parts, w, slots, width, size):
    tile = 512
    lone = len(slots) == 1
    rows = size if lone else WAYS * size
    outs, out_specs = slot_shapes(slots, size, width, tile)
    return call(
        functools.partial(back_project_kernel, lone, slots, size),
        (width // tile,),
        [whole((rows, p.shape[1]), (slots[0] if lone else 0, 0)) for p in parts]
        + [pl.BlockSpec((tile, 1024), lambda n: (n, 0))],
        outs,
        out_specs,
        flops=2 * len(slots) * size * width * 1024,
        size=10 << 20,
    )(*parts, w)


def attend_grads_kernel(n, q, k, v, w, out, gain_part):
    n_tile = n[...]
    at = 0
    total = jnp.zeros(gain_part.shape, f32)
    for ref in (q, k, v):
        cols = slice(at, at + ref.shape[1])
        product = tn(n_tile, ref[...])
        out[:, cols] = product.astype(bf16)
        total += jnp.sum(product * w[:, cols].astype(f32), axis=1, keepdims=True)
        at += ref.shape[1]
    out[:, at:] = jnp.zeros((out.shape[0], out.shape[1] - at), bf16)
    gain_part[...] = total


def attend_grads(normed, parts, w):
    rows, width = normed.shape
    tile = 512
    cols = sum(p.shape[1] for p in parts)
    return call(
        attend_grads_kernel,
        (width // tile,),
        [pl.BlockSpec((rows, tile), lambda j: (0, j))]
        + [whole(p.shape) for p in parts]
        + [pl.BlockSpec((tile, cols), lambda j: (j, 0))],
        [((width, cols + 128), bf16), ((width, 128), f32)],
        [pl.BlockSpec((tile, cols + 128), lambda j: (j, 0)), pl.BlockSpec((tile, 128), lambda j: (j, 0))],
        flops=2 * rows * width * 1024,
        size=16 << 20,
    )(normed, *parts, w)


def local(
    tokens,
    norm_attn,
    w_query,
    key_matrix,
    value_matrix,
    gain_query,
    gain_key,
    w_output,
    norm_ffn,
    w_gate,
    w_up,
    w_down,
    cotangent,
    lengths,
    deal_order,
):
    place = lax.axis_index("tensor")
    data_ways = lax.axis_size("dp")
    size, width = tokens.shape
    shard_rows = norm_attn.shape[0]
    gain_rows = gain_query.shape[0]
    q_width = w_query.shape[1]
    kv_width = key_matrix.shape[1]
    qkv_width = q_width + 2 * kv_width
    ff_width = w_gate.shape[1]
    place_ref = place.reshape(1).astype(jnp.int32)

    w_out = w_output.T
    x1, w1, w3 = together(hop(tokens), hop(w_out), shift_by(w_out, -1))
    offsets = jnp.arange(size, dtype=jnp.int32)
    position = jnp.concatenate([((place - j) % WAYS) * size + offsets for j in range(WAYS)])
    cos, sin = rope_tables(position)
    seq_len = sequence_length(lengths, deal_order, lax.axis_index("dp"))
    own_live = (position[:size] < seq_len).astype(f32)[:, None]
    d_branch = (cotangent.astype(f32) * own_live).astype(bf16)
    x2, w2, cos, sin, d_branch = together(hop(x1), hop(w1), cos, sin, d_branch)
    x3, d_branch = together(hop(x2), d_branch)
    x_slots = [tokens, x1, x2, x3]
    d1 = hop(d_branch)

    column = lambda v: jnp.pad(v, (0, shard_rows - v.shape[0]))[:, None]
    attn_part = jnp.concatenate(
        [w_query, key_matrix, value_matrix]
        + [column(v) for v in (norm_attn, norm_ffn, gain_query, gain_key)]
        + [jnp.zeros((shard_rows, 124), bf16)],
        axis=1,
    )
    attn_full = lax.all_gather(attn_part, "dp", axis=0, tiled=True)
    gain_block = attn_full[:, qkv_width : qkv_width + 4].astype(f32)
    norm_attn_all = gain_block[:, 0].reshape(1, width)
    norm_ffn_all = gain_block[:, 1].reshape(1, width)
    by_shard = gain_block.reshape(data_ways, shard_rows, 4)[:, :gain_rows]
    gain_q = by_shard[:, :, 2].reshape(1, HEAD_SIZE)
    gain_k = by_shard[:, :, 3].reshape(1, HEAD_SIZE)

    rest_full = lax.all_gather(
        jnp.concatenate([w_gate, w_up, w_out, w1, w2, w3], axis=1), "dp", axis=0, tiled=True
    )
    w_down_part, x2 = together(w_down.T, x2)
    x_slots = [tokens, x1, x2, x3]
    down_full = lax.all_gather(w_down_part, "dp", axis=0, tiled=True)

    normed_attn, qkv, pre = project(x_slots, attn_full, norm_attn_all, gain_q, gain_k, cos, sin)
    context, log_total = attend(place_ref, qkv)
    context, d1 = together(context, d1)
    c1 = hop(context)
    c2 = hop(c1)
    c3, d1 = together(hop(c2), d1)
    d2 = hop(d1)
    normed_ffn, hidden, ctx_rows = mix(x_slots, [context, c1, c2, c3], rest_full, norm_ffn_all)

    normed_ffn, d2 = together(normed_ffn, d2)
    d3 = hop(d2)
    forward = feed(normed_ffn, rest_full, ff_width)
    d_branch_all = jnp.concatenate([d_branch, d1, d2, d3], axis=0)
    grads_down = row_grads(d_branch_all, forward, 2, 1)
    forward, grads_down = together(forward, grads_down)
    grads_down = lax.psum_scatter(grads_down, "dp", scatter_dimension=0, tiled=True)
    y1, y2, y3, y0 = down(forward, down_full, (1, 2, 3, 0), width, size)
    y1, forward = together(y1, forward)
    y_sum = hop(y1)
    d_all = feed_back(d_branch_all, down_full, forward)
    (b1,) = back_feed(d_all, rest_full, (1,), width, size)
    b1, y_sum = together(b1, y_sum)
    b_sum = hop(b1)
    b2, b3, b0 = back_feed(d_all, rest_full, (2, 3, 0), width, size)
    b_sum, d_all = together(add(b2, b_sum), d_all)
    b_sum = hop(b_sum)
    grads_feed = row_grads(normed_ffn, d_all, 0, 2)
    b_sum, grads_feed = together(b_sum, grads_feed)
    grads_feed, grads_down = together(grads_feed, grads_down)
    grads_feed = lax.psum_scatter(grads_feed, "dp", scatter_dimension=0, tiled=True)
    b_sum, y_sum = together(hop(add(b3, b_sum)), y_sum)
    y_sum = hop(add(y2, y_sum))

    d_hidden, d_attended, p0, p1, p2, p3 = branch(
        (b0, b_sum), hidden, cotangent, own_live, norm_ffn_all, rest_full, q_width
    )
    grads_out = row_grads(d_attended, ctx_rows[None], 0, 1)
    s1, s2, s3, grads_out, y_sum = together(
        shift_by(p3, 1), shift_by(p2, 2), shift_by(p1, -1), grads_out, y_sum
    )
    d_q, d_k, d_v, sum_q, sum_k = attend_back(
        place_ref, qkv, [p0, s1, s2, s3], log_total, pre, cos, sin, gain_q, gain_k
    )
    (e1,) = back_project((d_q, d_k, d_v), attn_full, (1,), width, size)
    e1, d_q, grads_out, grads_feed = together(e1, d_q, grads_out, grads_feed)
    grads_out = lax.psum_scatter(grads_out, "dp", scatter_dimension=0, tiled=True)
    e_sum = hop(e1)
    y_sum = hop(add(y3, y_sum))
    parts = (d_q, d_k, d_v)
    e2, e3, e0 = back_project(parts, attn_full, (2, 3, 0), width, size)
    grads_attn, norm_part = attend_grads(normed_attn, parts, attn_full)
    e_sum, grads_attn, norm_part, y_sum = together(
        add(e2, e_sum), grads_attn, norm_part, y_sum
    )
    e_sum = hop(e_sum)
    own_ffn = jnp.sum(
        w_gate.astype(f32) * grads_feed[:, :ff_width].astype(f32)
        + w_up.astype(f32) * grads_feed[:, ff_width:].astype(f32),
        axis=1,
    ) / norm_ffn.astype(f32)
    small = jnp.concatenate(
        [
            norm_part[:, 0] / norm_attn_all[0],
            own_ffn,
            sum_q[0, :HEAD_SIZE] + sum_q[0, HEAD_SIZE:],
            sum_k[0, :HEAD_SIZE] + sum_k[0, HEAD_SIZE:],
        ]
    )
    small = small + shift_by(small, 1) + shift_by(small, 2) + shift_by(small, 3)
    grad_norm_ffn = small[width : width + shard_rows]
    gain_row = jnp.concatenate(
        [
            small[width + shard_rows :].reshape(2, data_ways, 1, gain_rows)[0],
            small[width + shard_rows :].reshape(2, data_ways, 1, gain_rows)[1],
            jnp.zeros((data_ways, 1, 127 - 2 * gain_rows), f32),
        ],
        axis=2,
    )
    gain_columns = jnp.concatenate(
        [
            small[:width].reshape(data_ways, shard_rows, 1),
            jnp.pad(gain_row, ((0, 0), (0, shard_rows - 1), (0, 0))),
        ],
        axis=2,
    ).reshape(width, 128).astype(bf16)
    grads_attn = lax.dynamic_update_slice(grads_attn, gain_columns, (0, qkv_width))
    grads_attn, grads_out, e_sum = together(grads_attn, grads_out, add(e3, e_sum))
    e_sum = hop(e_sum)
    grads_attn = lax.psum_scatter(grads_attn, "dp", scatter_dimension=0, tiled=True)
    d_normed_attn = e0.astype(f32) + e_sum.astype(f32)

    ffn_out = y0.astype(f32) + y_sum.astype(f32)
    block_out = ((hidden + ffn_out) * own_live).astype(bf16)
    own_tokens = tokens.astype(f32)
    d_tokens = d_hidden + norm_back(d_normed_attn, own_tokens, rms_scale(own_tokens), norm_attn_all)

    grads_feed = grads_feed.astype(f32)
    grad_gate, grad_up = grads_feed[:, :ff_width], grads_feed[:, ff_width:]
    grad_down = grads_down.astype(f32).T
    grad_qkv = grads_attn[:, :qkv_width].astype(f32)
    grad_query = grad_qkv[:, :q_width]
    grad_key = grad_qkv[:, q_width : q_width + kv_width]
    grad_value = grad_qkv[:, q_width + kv_width :]
    grad_norm_attn = grads_attn[:, qkv_width].astype(f32)
    gain_at = qkv_width + 1
    grad_gain_query = grads_attn[0, gain_at : gain_at + gain_rows].astype(f32)
    grad_gain_key = grads_attn[0, gain_at + gain_rows : gain_at + 2 * gain_rows].astype(f32)
    g0, g1, g2, g3 = [grads_out[:, k * q_width : (k + 1) * q_width] for k in range(WAYS)]
    g0, d_tokens = together(g0, d_tokens.astype(bf16))
    grad_output = (
        g0.astype(f32)
        + shift_by(g1, -1).astype(f32)
        + shift_by(g2, 2).astype(f32)
        + shift_by(g3, 1).astype(f32)
    ).T
    return (
        block_out,
        d_tokens,
        grad_norm_attn,
        grad_query,
        grad_key,
        grad_value,
        grad_gain_query,
        grad_gain_key,
        grad_output,
        grad_norm_ffn,
        grad_gate,
        grad_up,
        grad_down,
    )


def solution(mesh):
    return jax.shard_map(
        local,
        mesh=mesh,
        in_specs=(
            P(("dp", "tensor"), None),
            P("dp"),
            P("dp", "tensor"),
            P("dp", "tensor"),
            P("dp", "tensor"),
            P("dp"),
            P("dp"),
            P("tensor", "dp"),
            P("dp"),
            P("dp", "tensor"),
            P("dp", "tensor"),
            P("tensor", "dp"),
            P(("dp", "tensor"), None),
            P(),
            P(),
        ),
        out_specs=(
            P(("dp", "tensor"), None),
            P(("dp", "tensor"), None),
            P("dp"),
            P("dp", "tensor"),
            P("dp", "tensor"),
            P("dp", "tensor"),
            P("dp"),
            P("dp"),
            P("tensor", "dp"),
            P("dp"),
            P("dp", "tensor"),
            P("dp", "tensor"),
            P("tensor", "dp"),
        ),
        check_vma=False,
    )
```
